128 devices in a mesh: row: 8 (over x, core), col: 16 (over y, z).
Axes of the slice: x: 4, y: 4, z: 4, core: 2. Of those that a mesh axis runs over, the one named last changes fastest.
Arguments:
- tokens: bfloat16 [8, 1152, 8192], P('row', None, 'col'), may hold values from -64 to 64
- norm_gain: bfloat16 [8192], replicated, may hold values from 0.25 to 1.75
- w_query: bfloat16 [8192, 8192], P('row', 'col'), may hold values from -0.0625 to 0.0625
- w_keyval: bfloat16 [8192, 2048], P('row', 'col'), may hold values from -0.0625 to 0.0625
- kv_cache: bfloat16 [8, 8192, 2048], P('row', None, 'col'), may hold values from -96 to 96
- selected: int32 [8, 1152], P('row'), may hold values from 0 to 8192, as said below
- anchor: int32 [8, 16], P('row'), may hold values from 0 to 8191
Outputs:
- attended: bfloat16 [8, 1152, 8192], P('row', None, 'col')
The draws below stay inside these ranges and needn't reach their ends.
Inputs may be any that keep to these rules, and one draw needn't show every extreme that they name: Each prompt's row lists distinct positions in increasing order, followed by entries equal to 8192 in the unused slots; at least three quarters of the 1152 slots of a prompt are used and some prompt uses all of them; selected positions fall unevenly over the spans.
All inputs are finite; a program needn't handle non-finite values.
Results may differ from the reference program's by a relative error of at most 0.006.
The reference program's roundings to bfloat16 on the way count: a program that leaves them out, or rounds other values in their place, can miss the bound.
Values may be sent and summed in bfloat16 or wider, within the bound.
No kernel may reach another device: no remote copies, remote signals or barrier semaphores. Data moves between devices by JAX's collectives and lax.ppermute only.
A program may use at most 128 MiB of HBM per device.

```python
import math
import jax
import jax.numpy as jnp
from jax import lax

D = 8192
HQ = 64
KV = 8
HD = 128
SPAN = 512
NCHUNK = 16
S_MAX = 1152
P_SIZE = 8


def draw_tokens(key, part):
    first_key = jax.random.fold_in(key, 0)
    feature_ramp = jnp.exp(jnp.linspace(math.log(0.6), math.log(1.8), D))
    sampled = jax.random.normal(first_key, (P_SIZE, S_MAX, D), jnp.float32)
    return jnp.clip(sampled * feature_ramp, -64.0, 64.0).astype(jnp.bfloat16)


def draw_kv_cache(key, part):
    first_key = jax.random.fold_in(key, 0)
    sampled = jax.random.normal(first_key, (P_SIZE, NCHUNK * SPAN, 2 * KV * HD), jnp.float32)
    return jnp.clip(sampled, -96.0, 96.0).astype(jnp.bfloat16)


def draw_selected(key, part):
    first_key, second_key, third_key, fourth_key = jax.random.split(jax.random.fold_in(key, 7), 4)
    length = NCHUNK * SPAN
    span_weight = jax.random.randint(first_key, (P_SIZE, NCHUNK), 1, 9)
    noise = jax.random.randint(second_key, (P_SIZE, length), 0, 16384)
    scores = noise * jnp.repeat(span_weight, SPAN, axis=1) * length + jnp.arange(length, dtype=jnp.int32)[None, :]
    picked = lax.top_k(scores, S_MAX)[1].astype(jnp.int32)
    used = jax.random.randint(third_key, (P_SIZE,), 3 * S_MAX // 4, S_MAX + 1)
    full_prompt = jax.random.randint(fourth_key, (), 0, P_SIZE)
    used = jnp.where(jnp.arange(P_SIZE) == full_prompt, S_MAX, used)
    live = jnp.arange(S_MAX)[None, :] < used[:, None]
    picked = jnp.where(live, picked, length)
    return jnp.sort(picked, axis=1).astype(jnp.int32)


def with_ends(entries, own_key, low, largest):
    place = [jax.random.randint(jax.random.fold_in(own_key, axis), (), 0, length) for axis, length in enumerate(entries.shape)]
    main_axis = entries.shape.index(max(entries.shape))
    neighbour = place[:main_axis] + [(place[main_axis] + 1) % entries.shape[main_axis]] + place[main_axis + 1:]
    return entries.at[tuple(place)].set(low).at[tuple(neighbour)].set(largest)


def block_scale(rng, shape, cuts, least, largest):
    gain = 1.0
    for dim, blocks in cuts:
        steps = jax.random.uniform(jax.random.fold_in(jax.random.fold_in(rng, 6), dim), (blocks,), jnp.float32, least / len(cuts), largest / len(cuts))
        gain = gain * jnp.repeat(jnp.exp(steps), shape[dim] // blocks).reshape((-1,) + (1,) * (len(shape) - 1 - dim))
    return gain


def normal_values(key, dims, deviation, most, pieces=(), held_as=jnp.bfloat16):
    loudness = block_scale(key, dims, pieces, -0.22, 0.18) if pieces else 1.0
    values = jax.random.normal(key, dims, jnp.float32) * deviation * loudness
    return jnp.minimum(jnp.maximum(values, -most), most).astype(held_as)


def setup_inputs(seed: int = 0) -> dict:
    keys = jax.random.split(jax.random.key(seed), 8)
    tokens = draw_tokens(jax.random.fold_in(keys[7], 71), 0)
    norm_gain = jnp.clip(1.0 + 0.15 * jax.random.normal(keys[1], (D,), jnp.float32), 0.25, 1.75).astype(jnp.bfloat16)
    w_query = normal_values(keys[2], (D, HQ * HD), D ** -0.5, 0.0625, ((0, 8), (1, 16)))
    w_keyval = normal_values(keys[3], (D, 2 * KV * HD), D ** -0.5, 0.0625, ((0, 8), (1, 16)))
    kv_cache = draw_kv_cache(jax.random.fold_in(keys[7], 71), 0)
    selected = draw_selected(jax.random.fold_in(keys[7], 71), 0)
    anchor = with_ends(jax.random.randint(keys[6], (P_SIZE, NCHUNK), 0, NCHUNK * SPAN), jax.random.fold_in(keys[6], 1), 0, (NCHUNK * SPAN) - 1).astype(jnp.int32)
    return dict(tokens=tokens, norm_gain=norm_gain, w_query=w_query, w_keyval=w_keyval, kv_cache=kv_cache, selected=selected, anchor=anchor)


rope_base = 500000.0
epsilon = 1e-05
masked_score = -1e+30

def angles(positions, width):
    half_width = width // 2
    exponents = jnp.arange(half_width, dtype=jnp.float32) * (-2.0 / width)
    frequency = jnp.exp(exponents * math.log(rope_base))
    phases = positions[..., None] * frequency
    phases = jnp.concatenate([phases, phases], axis=-1)
    return (jnp.cos(phases), jnp.sin(phases))

def rotate(vectors, cosine, sine_part):
    half_width = vectors.shape[-1] // 2
    turned = jnp.concatenate([-vectors[..., half_width:], vectors[..., :half_width]], axis=-1)
    return vectors * cosine + turned * sine_part

def blend_rows(table, fresh, chosen):
    return table.at[chosen].set(fresh, mode='drop')

def reference(tokens, norm_gain, w_query, w_keyval, kv_cache, selected, anchor):
    hidden = tokens.astype(jnp.float32)
    mean_square = lax.optimization_barrier(jnp.mean(hidden * hidden, axis=-1, keepdims=True))
    normed = (hidden * lax.rsqrt(mean_square + epsilon) * norm_gain.astype(jnp.float32)).astype(jnp.bfloat16)
    flattened = normed.reshape(P_SIZE * S_MAX, D)
    queries = jnp.dot(flattened, w_query, preferred_element_type=jnp.float32).reshape(P_SIZE, S_MAX, HQ, HD)
    keyval = jnp.dot(flattened, w_keyval, preferred_element_type=jnp.float32).reshape(P_SIZE, S_MAX, KV, 2, HD)
    cosine, sine_part = angles(selected.astype(jnp.float32), HD)
    cosine = cosine[:, :, None]
    sine_part = sine_part[:, :, None]
    queries = rotate(queries, cosine, sine_part).astype(jnp.bfloat16)
    fresh_key = rotate(keyval[:, :, :, 0], cosine, sine_part).astype(jnp.bfloat16)
    fresh_value = keyval[:, :, :, 1].astype(jnp.bfloat16)
    length = NCHUNK * SPAN
    offsets = (jnp.arange(NCHUNK, dtype=jnp.int32) * SPAN)[None, :] - anchor.astype(jnp.int32)
    row_offsets = jnp.repeat(offsets, SPAN, axis=1).astype(jnp.float32)
    cache_cos, cache_sin = angles(row_offsets, HD)
    stored = kv_cache.reshape(P_SIZE, length, KV, 2, HD)
    key_rows = rotate(stored[:, :, :, 0].astype(jnp.float32), cache_cos[:, :, None], cache_sin[:, :, None]).astype(jnp.bfloat16)
    value_rows = stored[:, :, :, 1]
    key_rows = jax.vmap(blend_rows)(key_rows, fresh_key, selected)
    value_rows = jax.vmap(blend_rows)(value_rows, fresh_value, selected)
    group_size = HQ // KV
    scale = HD ** (-0.5)

    def attend_prompt(operands):
        queries_one, keys_one, values_one, chosen = operands
        visible = jnp.arange(length, dtype=jnp.int32)[None, :] <= chosen[:, None]

        def attend_head(head_index):
            query_head = lax.dynamic_index_in_dim(queries_one, head_index, 1, keepdims=False)
            key_head = lax.dynamic_index_in_dim(keys_one, head_index // group_size, 1, keepdims=False)
            value_head = lax.dynamic_index_in_dim(values_one, head_index // group_size, 1, keepdims=False)
            scores = jnp.dot(query_head, key_head.T, preferred_element_type=jnp.float32) * scale
            scores = jnp.where(visible, scores, masked_score)
            peak = lax.optimization_barrier(jnp.max(scores, axis=-1, keepdims=True))
            exponentials = jnp.exp(scores - peak)
            weights = exponentials.astype(jnp.bfloat16)
            numerator = jnp.dot(weights, value_head, preferred_element_type=jnp.float32)
            return numerator / lax.optimization_barrier(jnp.sum(exponentials, axis=-1, keepdims=True))
        per_head = lax.map(attend_head, jnp.arange(HQ, dtype=jnp.int32))
        return jnp.transpose(per_head, (1, 0, 2)).reshape(S_MAX, HQ * HD)
    attended = lax.map(attend_prompt, (queries, key_rows, value_rows, selected))
    live = (selected < length)[:, :, None]
    return jnp.where(live, attended, 0.0).astype(jnp.bfloat16)
```

```python
import functools
import math

import jax
import jax.numpy as jnp
from jax import lax
from jax.experimental import pallas as pl
from jax.experimental.pallas import tpu as pltpu
from jax.sharding import PartitionSpec as P

HD = 128
SPAN = 512
NCHUNK = 16
LENGTH = SPAN * NCHUNK
HEADS = 4
KEYS = 512
SLOTS = 128
HIDDEN_POSITION = 4 * LENGTH

rope_base = 500000.0
epsilon = 1e-05
masked_score = -1e30
exponent_scale = HD ** (-0.5) * math.log2(math.e)


def col_shift(dy, dz):
    return [(4 * y + z, 4 * ((y + dy) % 4) + (z + dz) % 4) for y in range(4) for z in range(4)]


def row_shift(dx):
    return [(2 * x + core, 2 * ((x + dx) % 4) + core) for x in range(4) for core in range(2)]


def flipped(count):
    return [(place, place ^ 1) for place in range(count)]


def angles(positions, width):
    half_width = width // 2
    exponents = jnp.arange(half_width, dtype=jnp.float32) * (-2.0 / width)
    frequency = jnp.exp(exponents * math.log(rope_base))
    phases = positions[..., None] * frequency
    cosine, sine_part = jnp.cos(phases), jnp.sin(phases)
    return (
        jnp.concatenate([cosine, cosine], axis=-1),
        jnp.concatenate([-sine_part, sine_part], axis=-1),
    )


def rotate(vectors, cosine, signed_sine):
    return vectors * cosine + pltpu.roll(vectors, HD // 2, 1) * signed_sine


def prepare_kernel(
    holds_key_ref, own_ref, partner_ref, cosine_ref, sine_ref, chosen_ref, key_ref, value_ref, place_ref
):
    step = pl.program_id(0)
    holds_key = holds_key_ref[0] == 1
    own = own_ref[...]
    partner = partner_ref[...]
    stored_key = jnp.where(holds_key, own, partner).astype(jnp.float32)
    stored_value = jnp.where(holds_key, partner, own).astype(jnp.float32)
    key_ref[...] = rotate(stored_key, cosine_ref[0], sine_ref[0]).astype(jnp.bfloat16)
    value_ref[...] = stored_value.T.astype(jnp.bfloat16)
    place = step * SPAN + lax.broadcasted_iota(jnp.int32, (SPAN, HD), 0)
    seen = jnp.zeros((SPAN, HD), jnp.int32)
    for start in range(0, chosen_ref.shape[1], HD):
        seen = jnp.where(place == chosen_ref[0:1, start : start + HD], 1, seen)
    replaced = jnp.max(seen, axis=1, keepdims=True) > 0
    place_ref[...] = jnp.where(replaced, HIDDEN_POSITION, place)


def prepare(holds_key, own, partner, cosine, signed_sine, chosen):
    block = pl.BlockSpec((SPAN, HD), lambda step, flag: (step, 0))
    angle = pl.BlockSpec((1, 1, HD), lambda step, flag: (step, 0, 0))
    return pl.pallas_call(
        prepare_kernel,
        out_shape=(
            jax.ShapeDtypeStruct((LENGTH, HD), jnp.bfloat16),
            jax.ShapeDtypeStruct((HD, LENGTH), jnp.bfloat16),
            jax.ShapeDtypeStruct((LENGTH, HD), jnp.int32),
        ),
        grid_spec=pltpu.PrefetchScalarGridSpec(
            num_scalar_prefetch=1,
            grid=(NCHUNK,),
            in_specs=[
                block,
                block,
                angle,
                angle,
                pl.BlockSpec((1, chosen.shape[1]), lambda step, flag: (0, 0)),
            ],
            out_specs=(
                block,
                pl.BlockSpec((HD, SPAN), lambda step, flag: (0, step)),
                block,
            ),
        ),
        cost_estimate=pl.CostEstimate(flops=10**7, bytes_accessed=12 * 2**20, transcendentals=0),
        name="prepare",
    )(holds_key, own, partner, cosine, signed_sine, chosen)


def project_kernel(pieces, place_ref, *refs):
    token_ref, gain_ref, cosine_ref, sine_ref = refs[:4]
    weight_refs = refs[4 : 4 + pieces]
    query_ref, key_ref, value_ref = refs[4 + pieces : 7 + pieces]
    held, weights, total, squares, token_sem, weight_sem = refs[7 + pieces :]
    blocks, slots, width = held.shape
    copies = [
        pltpu.make_async_copy(token_ref.at[block], held.at[block], token_sem.at[block])
        for block in range(blocks)
    ]
    for copy in copies:
        copy.start()
    weight_copies = []
    for piece, ref in enumerate(weight_refs):
        start = pl.multiple_of(place_ref[piece] * width, width)
        copy = pltpu.make_async_copy(
            ref, weights.at[pl.ds(start, ref.shape[0]), :], weight_sem.at[piece]
        )
        copy.start()
        weight_copies.append(copy)
    squares[...] = jnp.zeros_like(squares)
    for block in range(blocks):
        copies[block].wait()
        hidden = held[block].astype(jnp.float32)
        hidden = hidden * hidden
        part = hidden[:, :HD]
        for start in range(HD, width, HD):
            part = part + hidden[:, start : start + HD]
        squares[...] += part
    mean_square = jnp.sum(squares[...], axis=1, keepdims=True) * (1.0 / (blocks * width))
    squares[...] = jnp.broadcast_to(lax.rsqrt(mean_square + epsilon), squares.shape)
    for copy in weight_copies:
        copy.wait()
    total[...] = jnp.zeros_like(total)

    def add_block(block, carry):
        start = pl.multiple_of(block * width, width)
        scale = squares[:, 0:1]
        hidden = held[block].astype(jnp.float32) * scale * gain_ref[block].astype(jnp.float32)
        total[...] += jnp.dot(
            hidden.astype(jnp.bfloat16),
            weights[pl.ds(start, width), :],
            preferred_element_type=jnp.float32,
        )
        return carry

    lax.fori_loop(0, blocks, add_block, 0)
    cosine, signed_sine = cosine_ref[...], sine_ref[...]
    for head in range(HEADS):
        part = total[:, head * HD : (head + 1) * HD]
        query_ref[head] = rotate(part, cosine, signed_sine).astype(jnp.bfloat16)
    key_ref[...] = rotate(total[:, HEADS * HD : (HEADS + 1) * HD], cosine, signed_sine).astype(
        jnp.bfloat16
    )
    value_ref[...] = total[:, (HEADS + 1) * HD :].T.astype(jnp.bfloat16)


def project(tokens, gain, cosine, signed_sine, weight_pieces, places):
    blocks, slots, width = tokens.shape
    columns = (HEADS + 2) * HD
    pieces = len(weight_pieces)
    whole = pl.BlockSpec(memory_space=pltpu.VMEM)
    remote = pl.BlockSpec(memory_space=pl.ANY)
    return pl.pallas_call(
        functools.partial(project_kernel, pieces),
        out_shape=(
            jax.ShapeDtypeStruct((HEADS, slots, HD), jnp.bfloat16),
            jax.ShapeDtypeStruct((slots, HD), jnp.bfloat16),
            jax.ShapeDtypeStruct((HD, slots), jnp.bfloat16),
        ),
        in_specs=[pl.BlockSpec(memory_space=pltpu.SMEM), remote, whole, whole, whole]
        + [remote] * pieces,
        out_specs=(whole, whole, whole),
        scratch_shapes=[
            pltpu.VMEM((blocks, slots, width), jnp.bfloat16),
            pltpu.VMEM((blocks * width, columns), jnp.bfloat16),
            pltpu.VMEM((slots, columns), jnp.float32),
            pltpu.VMEM((slots, HD), jnp.float32),
            pltpu.SemaphoreType.DMA((blocks,)),
            pltpu.SemaphoreType.DMA((pieces,)),
        ],
        compiler_params=pltpu.CompilerParams(vmem_limit_bytes=58 * 2**20),
        cost_estimate=pl.CostEstimate(
            flops=2 * slots * blocks * width * columns,
            bytes_accessed=2 * blocks * width * (slots + columns),
            transcendentals=0,
        ),
        name="project",
    )(places, tokens, gain, cosine, signed_sine, *weight_pieces)


def attend_kernel(
    first,
    blocks_ref,
    query_ref,
    chosen_ref,
    key_ref,
    value_ref,
    place_ref,
    fresh_key_ref,
    fresh_value_ref,
    fresh_place_ref,
    out_ref,
    peak,
    denominator,
    numerator,
    held,
):
    step = pl.program_id(0)
    rows = HEADS * SLOTS
    peak[...] = jnp.full_like(peak, masked_score)
    denominator[...] = jnp.zeros_like(denominator)
    numerator[...] = jnp.zeros_like(numerator)
    queries = query_ref[...].reshape(rows, HD)
    limit = jnp.concatenate([chosen_ref[...]] * HEADS, axis=1)

    def score(keys, block, slot):
        start = pl.multiple_of(block * KEYS, KEYS)
        held[slot] = lax.dot_general(
            keys[pl.ds(start, KEYS), :],
            queries,
            (((1,), (1,)), ((), ())),
            preferred_element_type=jnp.float32,
        )

    def gather(values, places, block, slot):
        start = pl.multiple_of(block * KEYS, KEYS)
        place = jnp.concatenate([places[pl.ds(start, KEYS), :]] * HEADS, axis=1)
        scores = jnp.where(place <= limit, held[slot], masked_score)
        old_peak = peak[...]
        new_peak = jnp.maximum(old_peak, jnp.max(scores, axis=0, keepdims=True))
        rescale = jnp.exp2((old_peak - new_peak) * exponent_scale)
        weights = jnp.exp2((scores - new_peak) * exponent_scale)
        denominator[...] = denominator[...] * rescale + jnp.sum(weights, axis=0, keepdims=True)
        numerator[...] = numerator[...] * rescale + jnp.dot(
            values[:, pl.ds(start, KEYS)],
            weights.astype(jnp.bfloat16),
            preferred_element_type=jnp.float32,
        )
        peak[...] = new_peak

    def walk(keys, values, places, count):
        last = jnp.maximum(count - 1, 0)
        score(keys, 0, 0)

        def pair(turn, carry):
            block = 2 * turn
            score(keys, jnp.minimum(block + 1, last), 1)
            gather(values, places, block, 0)
            score(keys, jnp.minimum(block + 2, last), 0)
            gather(values, places, block + 1, 1)
            return carry

        lax.fori_loop(0, count // 2, pair, 0)

        @pl.when(count % 2 == 1)
        def _():
            gather(values, places, count - 1, 0)

    walk(key_ref, value_ref, place_ref, blocks_ref[step])
    walk(
        fresh_key_ref,
        fresh_value_ref,
        fresh_place_ref,
        ((first + step + 1) * SLOTS + KEYS - 1) // KEYS,
    )
    outcome = jnp.where(limit < LENGTH, numerator[...] / denominator[...], 0.0)
    for head in range(HEADS):
        part = outcome[:, head * SLOTS : (head + 1) * SLOTS]
        out_ref[:, head * HD : (head + 1) * HD] = part.T.astype(jnp.bfloat16)


def attend(first, key_blocks, queries, chosen, keys, values, places, fresh_keys, fresh_values, fresh_places):
    slots = queries.shape[1]
    rows = HEADS * SLOTS

    def still(array):
        return pl.BlockSpec(
            array.shape, lambda step, counts: (0, 0), pipeline_mode=pl.Buffered(1)
        )

    return pl.pallas_call(
        functools.partial(attend_kernel, first),
        out_shape=jax.ShapeDtypeStruct((slots, HEADS * HD), jnp.bfloat16),
        grid_spec=pltpu.PrefetchScalarGridSpec(
            num_scalar_prefetch=1,
            grid=(slots // SLOTS,),
            in_specs=[
                pl.BlockSpec((HEADS, SLOTS, HD), lambda step, counts: (0, step, 0)),
                pl.BlockSpec((1, SLOTS), lambda step, counts: (0, step)),
                still(keys),
                still(values),
                still(places),
                still(fresh_keys),
                still(fresh_values),
                still(fresh_places),
            ],
            out_specs=pl.BlockSpec((SLOTS, HEADS * HD), lambda step, counts: (step, 0)),
            scratch_shapes=[
                pltpu.VMEM((1, rows), jnp.float32),
                pltpu.VMEM((1, rows), jnp.float32),
                pltpu.VMEM((HD, rows), jnp.float32),
                pltpu.VMEM((2, KEYS, rows), jnp.float32),
            ],
        ),
        compiler_params=pltpu.CompilerParams(vmem_limit_bytes=48 * 2**20),
        cost_estimate=pl.CostEstimate(
            flops=slots * HEADS * LENGTH * HD * 2,
            bytes_accessed=12 * 2**20,
            transcendentals=slots * HEADS * LENGTH // 2,
        ),
        name="attend",
    )(key_blocks, queries, chosen, keys, values, places, fresh_keys, fresh_values, fresh_places)


def shards(tokens, norm_gain, w_query, w_keyval, kv_cache, selected, anchor):
    row_index = lax.axis_index("row")
    col_index = lax.axis_index("col")
    own_x, own_core = row_index // 2, row_index % 2
    holds_key = col_index % 2 == 0
    own_cache = kv_cache[0]
    other_keyval = lax.ppermute(w_keyval, "col", flipped(16))
    other_cache = lax.ppermute(own_cache, "col", flipped(16))
    gathered = lax.all_gather(tokens[0], "col", axis=0)

    weights = jnp.concatenate(
        [
            w_query,
            jnp.where(holds_key, w_keyval, other_keyval),
            jnp.where(holds_key, other_keyval, w_keyval),
        ],
        axis=1,
    )
    half = weights.shape[0] // 2
    behind = lax.ppermute(weights, "row", row_shift(1))
    ahead = lax.ppermute(weights, "row", row_shift(-1))
    far_first = lax.ppermute(behind[:half], "row", row_shift(1))
    far_second = lax.ppermute(ahead[half:], "row", row_shift(-1))
    mine = [weights, behind, ahead, far_first, far_second]
    theirs = [lax.ppermute(piece, "row", flipped(8)) for piece in mine]
    steps_x = jnp.array([0, 3, 1, 2, 2], jnp.int32)
    second_half = jnp.array([0, 0, 0, 0, 1], jnp.int32)
    source_x = (own_x + steps_x) % 4
    places = jnp.concatenate(
        [
            (source_x * 2 + own_core) * 2 + second_half,
            (source_x * 2 + 1 - own_core) * 2 + second_half,
        ]
    )

    chosen = selected[0]
    slot_count = chosen.shape[0]
    cosine, signed_sine = angles(chosen.astype(jnp.float32), HD)
    offsets = jnp.arange(NCHUNK, dtype=jnp.int32) * SPAN - anchor[0]
    span_cosine, span_sine = angles(offsets.astype(jnp.float32), HD)
    keys, values, key_places = prepare(
        holds_key.astype(jnp.int32)[None],
        own_cache,
        other_cache,
        span_cosine[:, None],
        span_sine[:, None],
        chosen[None],
    )
    grouped = chosen.reshape(-1, SLOTS)
    farthest = jnp.max(jnp.where(grouped < LENGTH, grouped, -1), axis=1)
    key_blocks = (farthest + KEYS) // KEYS
    padded = -(-slot_count // KEYS) * KEYS - slot_count
    fresh_places = jnp.broadcast_to(
        jnp.pad(chosen, (0, padded), constant_values=HIDDEN_POSITION)[:, None],
        (slot_count + padded, HD),
    )

    gain = norm_gain.reshape(NCHUNK, 1, -1)
    queries, fresh_keys, fresh_values = project(
        gathered, gain, cosine, signed_sine, mine + theirs, places
    )
    fresh_keys = jnp.pad(fresh_keys, ((0, padded), (0, 0)))
    fresh_values = jnp.pad(fresh_values, ((0, 0), (0, padded)))
    attended = attend(
        0, key_blocks, queries, chosen[None], keys, values, key_places, fresh_keys, fresh_values, fresh_places
    )
    return attended[None]


def solution(mesh):
    in_specs = (
        P("row", None, "col"),
        P(),
        P("row", "col"),
        P("row", "col"),
        P("row", None, "col"),
        P("row", None),
        P("row", None),
    )
    out_specs = P("row", None, "col")
    return jax.shard_map(shards, mesh=mesh, in_specs=in_specs, out_specs=out_specs, check_vma=False)
```

```python
import functools
import math

import jax
import jax.numpy as jnp
from jax import lax
from jax.experimental import pallas as pl
from jax.experimental.pallas import tpu as pltpu
from jax.sharding import PartitionSpec as P

HD = 128
SPAN = 512
NCHUNK = 16
LENGTH = SPAN * NCHUNK
HEADS = 4
KEYS = 512
SLOTS = 128
HIDDEN_POSITION = 4 * LENGTH
EARLY = 5
Y_FIRST = 2

rope_base = 500000.0
epsilon = 1e-05
masked_score = -1e30
exponent_scale = HD ** (-0.5) * math.log2(math.e)


def col_shift(dy, dz):
    return [(4 * y + z, 4 * ((y + dy) % 4) + (z + dz) % 4) for y in range(4) for z in range(4)]


def row_shift(dx):
    return [(2 * x + core, 2 * ((x + dx) % 4) + core) for x in range(4) for core in range(2)]


def flipped(count):
    return [(place, place ^ 1) for place in range(count)]


def angles(positions, width):
    half_width = width // 2
    exponents = jnp.arange(half_width, dtype=jnp.float32) * (-2.0 / width)
    frequency = jnp.exp(exponents * math.log(rope_base))
    phases = positions[..., None] * frequency
    cosine, sine_part = jnp.cos(phases), jnp.sin(phases)
    return (
        jnp.concatenate([cosine, cosine], axis=-1),
        jnp.concatenate([-sine_part, sine_part], axis=-1),
    )


def rotate(vectors, cosine, signed_sine):
    return vectors * cosine + pltpu.roll(vectors, HD // 2, 1) * signed_sine


def prepare_kernel(
    holds_key_ref, own_ref, partner_ref, cosine_ref, sine_ref, chosen_ref, key_ref, value_ref, place_ref
):
    step = pl.program_id(0)
    holds_key = holds_key_ref[0] == 1
    own = own_ref[...]
    partner = partner_ref[...]
    stored_key = jnp.where(holds_key, own, partner).astype(jnp.float32)
    stored_value = jnp.where(holds_key, partner, own).astype(jnp.float32)
    key_ref[...] = rotate(stored_key, cosine_ref[0], sine_ref[0]).astype(jnp.bfloat16)
    value_ref[...] = stored_value.T.astype(jnp.bfloat16)
    place = step * SPAN + lax.broadcasted_iota(jnp.int32, (SPAN, HD), 0)
    seen = jnp.zeros((SPAN, HD), jnp.int32)
    for start in range(0, chosen_ref.shape[1], HD):
        seen = jnp.where(place == chosen_ref[0:1, start : start + HD], 1, seen)
    replaced = jnp.max(seen, axis=1, keepdims=True) > 0
    place_ref[...] = jnp.where(replaced, HIDDEN_POSITION, place)


def prepare(holds_key, own, partner, cosine, signed_sine, chosen):
    block = pl.BlockSpec((SPAN, HD), lambda step, flag: (step, 0))
    angle = pl.BlockSpec((1, 1, HD), lambda step, flag: (step, 0, 0))
    return pl.pallas_call(
        prepare_kernel,
        out_shape=(
            jax.ShapeDtypeStruct((LENGTH, HD), jnp.bfloat16),
            jax.ShapeDtypeStruct((HD, LENGTH), jnp.bfloat16),
            jax.ShapeDtypeStruct((LENGTH, HD), jnp.int32),
        ),
        grid_spec=pltpu.PrefetchScalarGridSpec(
            num_scalar_prefetch=1,
            grid=(NCHUNK,),
            in_specs=[
                block,
                block,
                angle,
                angle,
                pl.BlockSpec((1, chosen.shape[1]), lambda step, flag: (0, 0)),
            ],
            out_specs=(
                block,
                pl.BlockSpec((HD, SPAN), lambda step, flag: (0, step)),
                block,
            ),
        ),
        cost_estimate=pl.CostEstimate(flops=10**7, bytes_accessed=12 * 2**20, transcendentals=0),
        name="prepare",
    )(holds_key, own, partner, cosine, signed_sine, chosen)


def project_kernel(offsets, token_count, weight_count, done, *refs):
    token_place_ref, weight_place_ref, gain_ref, cosine_ref, sine_ref, old_key_ref, old_value_ref = refs[:7]
    refs = refs[7:]
    token_refs, refs = refs[:token_count], refs[token_count:]
    weight_refs, refs = refs[:weight_count], refs[weight_count:]
    query_ref, key_ref, value_ref, held, weights, total, squares, token_sem, weight_sem = refs
    blocks, slots, width = held.shape
    token_copies = []
    for piece, ref in enumerate(token_refs):
        for part in range(ref.shape[0]):
            number = len(token_copies)
            where = held.at[token_place_ref[number], pl.ds(offsets[piece], ref.shape[1]), :]
            token_copies.append(pltpu.make_async_copy(ref.at[part], where, token_sem.at[number]))
    weight_copies = []
    for piece, ref in enumerate(weight_refs):
        start = pl.multiple_of(weight_place_ref[piece] * width, width)
        where = weights.at[pl.ds(start, ref.shape[0]), :]
        weight_copies.append(pltpu.make_async_copy(ref, where, weight_sem.at[piece]))
    for copy in token_copies + weight_copies:
        copy.start()
    for copy in token_copies:
        copy.wait()
    squares[...] = jnp.zeros_like(squares)

    def add_squares(block, carry):
        hidden = held[block].astype(jnp.float32)
        hidden = hidden * hidden
        part = hidden[:, :HD]
        for start in range(HD, width, HD):
            part = part + hidden[:, start : start + HD]
        squares[...] += part
        return carry

    lax.fori_loop(0, blocks, add_squares, 0)
    mean_square = jnp.sum(squares[...], axis=1, keepdims=True) * (1.0 / (blocks * width))
    squares[...] = jnp.broadcast_to(lax.rsqrt(mean_square + epsilon), squares.shape)
    for copy in weight_copies:
        copy.wait()
    total[...] = jnp.zeros_like(total)

    def add_block(block, carry):
        start = pl.multiple_of(block * width, width)
        scale = jnp.concatenate([squares[...]] * (width // HD), axis=1)
        hidden = held[block].astype(jnp.float32) * scale * gain_ref[block].astype(jnp.float32)
        total[...] += jnp.dot(
            hidden.astype(jnp.bfloat16),
            weights[pl.ds(start, width), :],
            preferred_element_type=jnp.float32,
        )
        return carry

    lax.fori_loop(0, blocks, add_block, 0)
    cosine, signed_sine = cosine_ref[...], sine_ref[...]
    for head in range(HEADS):
        part = total[:, head * HD : (head + 1) * HD]
        query_ref[head] = rotate(part, cosine, signed_sine).astype(jnp.bfloat16)
    if done:
        key_ref[:done, :] = old_key_ref[:done, :]
        value_ref[:, :done] = old_value_ref[:, :done]
    key_ref[done : done + slots, :] = rotate(
        total[:, HEADS * HD : (HEADS + 1) * HD], cosine, signed_sine
    ).astype(jnp.bfloat16)
    value_ref[:, done : done + slots] = total[:, (HEADS + 1) * HD :].T.astype(jnp.bfloat16)
    if done + slots < key_ref.shape[0]:
        key_ref[done + slots :, :] = jnp.zeros_like(key_ref[done + slots :, :])
        value_ref[:, done + slots :] = jnp.zeros_like(value_ref[:, done + slots :])


def project(token_pieces, offsets, token_places, gain, cosine, signed_sine, weight_pieces, weight_places, done, old):
    slots = cosine.shape[0]
    width = token_pieces[0].shape[-1]
    blocks = gain.shape[0]
    columns = (HEADS + 2) * HD
    fresh = -(-(done + slots) // KEYS) * KEYS
    whole = pl.BlockSpec(memory_space=pltpu.VMEM)
    remote = pl.BlockSpec(memory_space=pl.ANY)
    scalars = pl.BlockSpec(memory_space=pltpu.SMEM)
    return pl.pallas_call(
        functools.partial(project_kernel, offsets, len(token_pieces), len(weight_pieces), done),
        out_shape=(
            jax.ShapeDtypeStruct((HEADS, slots, HD), jnp.bfloat16),
            jax.ShapeDtypeStruct((fresh, HD), jnp.bfloat16),
            jax.ShapeDtypeStruct((HD, fresh), jnp.bfloat16),
        ),
        in_specs=[scalars, scalars, whole, whole, whole, whole, whole]
        + [remote] * (len(token_pieces) + len(weight_pieces)),
        out_specs=(whole, whole, whole),
        scratch_shapes=[
            pltpu.VMEM((blocks, slots, width), jnp.bfloat16),
            pltpu.VMEM((blocks * width, columns), jnp.bfloat16),
            pltpu.VMEM((slots, columns), jnp.float32),
            pltpu.VMEM((slots, HD), jnp.float32),
            pltpu.SemaphoreType.DMA((token_places.shape[0],)),
            pltpu.SemaphoreType.DMA((len(weight_pieces),)),
        ],
        compiler_params=pltpu.CompilerParams(vmem_limit_bytes=48 * 2**20),
        cost_estimate=pl.CostEstimate(
            flops=4 * slots * blocks * width * columns,
            bytes_accessed=2 * blocks * width * (slots + columns),
            transcendentals=0,
        ),
        name="project",
    )(token_places, weight_places, gain, cosine, signed_sine, *old, *token_pieces, *weight_pieces)


def attend_kernel(
    first,
    blocks_ref,
    query_ref,
    chosen_ref,
    key_ref,
    value_ref,
    place_ref,
    fresh_key_ref,
    fresh_value_ref,
    fresh_place_ref,
    out_ref,
    peak,
    denominator,
    numerator,
    held,
):
    step = pl.program_id(0)
    rows = HEADS * SLOTS
    peak[...] = jnp.full_like(peak, masked_score)
    denominator[...] = jnp.zeros_like(denominator)
    numerator[...] = jnp.zeros_like(numerator)
    queries = query_ref[...].reshape(rows, HD)
    limit = jnp.concatenate([chosen_ref[...]] * HEADS, axis=1)

    def score(keys, block, slot):
        start = pl.multiple_of(block * KEYS, KEYS)
        held[slot] = lax.dot_general(
            keys[pl.ds(start, KEYS), :],
            queries,
            (((1,), (1,)), ((), ())),
            preferred_element_type=jnp.float32,
        )

    def gather(values, places, block, slot):
        start = pl.multiple_of(block * KEYS, KEYS)
        place = jnp.concatenate([places[pl.ds(start, KEYS), :]] * HEADS, axis=1)
        scores = jnp.where(place <= limit, held[slot], masked_score)
        old_peak = peak[...]
        new_peak = jnp.maximum(old_peak, jnp.max(scores, axis=0, keepdims=True))
        rescale = jnp.exp2((old_peak - new_peak) * exponent_scale)
        weights = jnp.exp2((scores - new_peak) * exponent_scale)
        denominator[...] = denominator[...] * rescale + jnp.sum(weights, axis=0, keepdims=True)
        numerator[...] = numerator[...] * rescale + jnp.dot(
            values[:, pl.ds(start, KEYS)],
            weights.astype(jnp.bfloat16),
            preferred_element_type=jnp.float32,
        )
        peak[...] = new_peak

    def walk(keys, values, places, count):
        last = jnp.maximum(count - 1, 0)
        score(keys, 0, 0)

        def pair(turn, carry):
            block = 2 * turn
            score(keys, jnp.minimum(block + 1, last), 1)
            gather(values, places, block, 0)
            score(keys, jnp.minimum(block + 2, last), 0)
            gather(values, places, block + 1, 1)
            return carry

        lax.fori_loop(0, count // 2, pair, 0)

        @pl.when(count % 2 == 1)
        def _():
            gather(values, places, count - 1, 0)

    walk(key_ref, value_ref, place_ref, blocks_ref[step])
    walk(
        fresh_key_ref,
        fresh_value_ref,
        fresh_place_ref,
        ((first + step + 1) * SLOTS + KEYS - 1) // KEYS,
    )
    outcome = jnp.where(limit < LENGTH, numerator[...] / denominator[...], 0.0)
    for head in range(HEADS):
        part = outcome[:, head * SLOTS : (head + 1) * SLOTS]
        out_ref[:, head * HD : (head + 1) * HD] = part.T.astype(jnp.bfloat16)


def attend(first, key_blocks, queries, chosen, keys, values, places, fresh_keys, fresh_values, fresh_places):
    slots = queries.shape[1]
    rows = HEADS * SLOTS

    def still(array):
        return pl.BlockSpec(
            array.shape, lambda step, counts: (0, 0), pipeline_mode=pl.Buffered(1)
        )

    return pl.pallas_call(
        functools.partial(attend_kernel, first),
        out_shape=jax.ShapeDtypeStruct((slots, HEADS * HD), jnp.bfloat16),
        grid_spec=pltpu.PrefetchScalarGridSpec(
            num_scalar_prefetch=1,
            grid=(slots // SLOTS,),
            in_specs=[
                pl.BlockSpec((HEADS, SLOTS, HD), lambda step, counts: (0, step, 0)),
                pl.BlockSpec((1, SLOTS), lambda step, counts: (0, step)),
                still(keys),
                still(values),
                still(places),
                still(fresh_keys),
                still(fresh_values),
                still(fresh_places),
            ],
            out_specs=pl.BlockSpec((SLOTS, HEADS * HD), lambda step, counts: (step, 0)),
            scratch_shapes=[
                pltpu.VMEM((1, rows), jnp.float32),
                pltpu.VMEM((1, rows), jnp.float32),
                pltpu.VMEM((HD, rows), jnp.float32),
                pltpu.VMEM((2, KEYS, rows), jnp.float32),
            ],
        ),
        compiler_params=pltpu.CompilerParams(vmem_limit_bytes=48 * 2**20),
        cost_estimate=pl.CostEstimate(
            flops=slots * HEADS * LENGTH * HD * 2,
            bytes_accessed=12 * 2**20,
            transcendentals=slots * HEADS * LENGTH // 2,
        ),
        name="attend",
    )(key_blocks, queries, chosen, keys, values, places, fresh_keys, fresh_values, fresh_places)


def ring(block, axis, shift):
    half = block.shape[-2] // 2
    behind = lax.ppermute(block, axis, shift(1))
    ahead = lax.ppermute(block, axis, shift(-1))
    far_first = lax.ppermute(behind[..., :half, :], axis, shift(1))
    far_second = lax.ppermute(ahead[..., half:, :], axis, shift(-1))
    return [block, behind, ahead, far_first, far_second]


def stacked(pieces):
    far = jnp.concatenate(pieces[3:], axis=-2)
    return jnp.stack([*pieces[:3], far])


def along_y(steps):
    return col_shift(steps, 0)


def along_z(steps):
    return col_shift(0, steps)


def gather_by_permutes(part, y_first):
    col_index = lax.axis_index("col")
    own_y, own_z = col_index // 4, col_index % 4
    slots = part.shape[0]
    cut = y_first * SLOTS
    near = jnp.array([0, 3, 1, 2], jnp.int32)[None, :]
    far = jnp.array([0, 3, 1, 2, 2], jnp.int32)[:, None]
    over_y = stacked(ring(part[:cut], "col", along_y))
    over_z = stacked(ring(part[cut:], "col", along_z))
    pieces = ring(over_y, "col", along_z) + ring(over_z, "col", along_y)
    first = (own_y + near) % 4 * 4 + (own_z + far) % 4
    second = (own_y + far) % 4 * 4 + (own_z + near) % 4
    places = jnp.concatenate([first.reshape(-1), second.reshape(-1)])
    middle = cut + (slots - cut) // 2
    offsets = (0, 0, 0, 0, cut // 2, cut, cut, cut, cut, middle)
    return pieces, offsets, places


def shards(tokens, norm_gain, w_query, w_keyval, kv_cache, selected, anchor):
    row_index = lax.axis_index("row")
    col_index = lax.axis_index("col")
    own_x, own_core = row_index // 2, row_index % 2
    holds_key = col_index % 2 == 0
    own_cache = kv_cache[0]
    chosen = selected[0]
    slot_count = chosen.shape[0]
    early = EARLY * SLOTS
    other_keyval = lax.ppermute(w_keyval, "col", flipped(16))
    late_tokens = lax.all_gather(tokens[0, early:], "col", axis=0)
    early_pieces, offsets, early_places = gather_by_permutes(tokens[0, :early], Y_FIRST)
    other_cache = lax.ppermute(own_cache, "col", flipped(16))

    weights = jnp.concatenate(
        [
            w_query,
            jnp.where(holds_key, w_keyval, other_keyval),
            jnp.where(holds_key, other_keyval, w_keyval),
        ],
        axis=1,
    )
    mine = ring(weights, "row", row_shift)
    theirs = [lax.ppermute(piece, "row", flipped(8)) for piece in mine]
    steps_x = jnp.array([0, 3, 1, 2, 2], jnp.int32)
    second_half = jnp.array([0, 0, 0, 0, 1], jnp.int32)
    source_x = (own_x + steps_x) % 4
    weight_places = jnp.concatenate(
        [
            (source_x * 2 + own_core) * 2 + second_half,
            (source_x * 2 + 1 - own_core) * 2 + second_half,
        ]
    )

    cosine, signed_sine = angles(chosen.astype(jnp.float32), HD)
    span_starts = jnp.arange(NCHUNK, dtype=jnp.int32) * SPAN - anchor[0]
    span_cosine, span_sine = angles(span_starts.astype(jnp.float32), HD)
    keys, values, key_places = prepare(
        holds_key.astype(jnp.int32)[None],
        own_cache,
        other_cache,
        span_cosine[:, None],
        span_sine[:, None],
        chosen[None],
    )
    grouped = chosen.reshape(-1, SLOTS)
    farthest = jnp.max(jnp.where(grouped < LENGTH, grouped, -1), axis=1)
    key_blocks = (farthest + KEYS) // KEYS
    padded = -(-slot_count // KEYS) * KEYS - slot_count
    fresh_places = jnp.broadcast_to(
        jnp.pad(chosen, (0, padded), constant_values=HIDDEN_POSITION)[:, None],
        (slot_count + padded, HD),
    )
    gain = norm_gain.reshape(NCHUNK, 1, -1)
    nothing = (jnp.zeros((16, HD), jnp.bfloat16), jnp.zeros((16, HD), jnp.bfloat16))
    absolute = jnp.arange(NCHUNK, dtype=jnp.int32)
    results = []
    fresh = nothing
    for start, stop, pieces, piece_offsets, piece_places in (
        (0, early, early_pieces, offsets, early_places),
        (early, slot_count, [late_tokens], (0,), absolute),
    ):
        queries, *fresh = project(
            pieces,
            piece_offsets,
            piece_places,
            gain,
            cosine[start:stop],
            signed_sine[start:stop],
            mine + theirs,
            weight_places,
            start,
            fresh,
        )
        results.append(
            attend(
                start // SLOTS,
                key_blocks[start // SLOTS : stop // SLOTS],
                queries,
                chosen[None, start:stop],
                keys,
                values,
                key_places,
                *fresh,
                fresh_places,
            )
        )
    return jnp.concatenate(results, axis=0)[None]


def solution(mesh):
    in_specs = (
        P("row", None, "col"),
        P(),
        P("row", "col"),
        P("row", "col"),
        P("row", None, "col"),
        P("row", None),
        P("row", None),
    )
    out_specs = P("row", None, "col")
    return jax.shard_map(shards, mesh=mesh, in_specs=in_specs, out_specs=out_specs, check_vma=False)
```

```python
import functools
import math

import jax
import jax.numpy as jnp
from jax import lax
from jax.experimental import pallas as pl
from jax.experimental.pallas import tpu as pltpu
from jax.sharding import PartitionSpec as P

HD = 128
SPAN = 512
NCHUNK = 16
LENGTH = SPAN * NCHUNK
HEADS = 4
KEYS = 512
SLOTS = 128
HIDDEN_POSITION = 4 * LENGTH
EARLY = 6
TILE = 64
ROWS = 384
GROUP = 4

rope_base = 500000.0
epsilon = 1e-05
masked_score = -1e30
exponent_scale = HD ** (-0.5) * math.log2(math.e)


def col_shift(dy, dz):
    return [(4 * y + z, 4 * ((y + dy) % 4) + (z + dz) % 4) for y in range(4) for z in range(4)]


def row_shift(dx):
    return [(2 * x + core, 2 * ((x + dx) % 4) + core) for x in range(4) for core in range(2)]


def flipped(count):
    return [(place, place ^ 1) for place in range(count)]


def angles(positions, width):
    half_width = width // 2
    exponents = jnp.arange(half_width, dtype=jnp.float32) * (-2.0 / width)
    frequency = jnp.exp(exponents * math.log(rope_base))
    phases = positions[..., None] * frequency
    cosine, sine_part = jnp.cos(phases), jnp.sin(phases)
    return (
        jnp.concatenate([cosine, cosine], axis=-1),
        jnp.concatenate([-sine_part, sine_part], axis=-1),
    )


def rotate(vectors, cosine, signed_sine):
    return vectors * cosine + pltpu.roll(vectors, HD // 2, 1) * signed_sine


def prepare_kernel(
    holds_key_ref, own_ref, partner_ref, cosine_ref, sine_ref, chosen_ref, key_ref, value_ref, place_ref
):
    step = pl.program_id(0)
    holds_key = holds_key_ref[0] == 1
    own = own_ref[...]
    partner = partner_ref[...]
    stored_key = jnp.where(holds_key, own, partner).astype(jnp.float32)
    stored_value = jnp.where(holds_key, partner, own).astype(jnp.float32)
    key_ref[...] = rotate(stored_key, cosine_ref[0], sine_ref[0]).astype(jnp.bfloat16)
    value_ref[...] = stored_value.T.astype(jnp.bfloat16)
    place = step * SPAN + lax.broadcasted_iota(jnp.int32, (SPAN, HD), 0)
    seen = jnp.zeros((SPAN, HD), jnp.int32)
    for start in range(0, chosen_ref.shape[1], HD):
        seen = jnp.where(place == chosen_ref[0:1, start : start + HD], 1, seen)
    replaced = jnp.max(seen, axis=1, keepdims=True) > 0
    place_ref[...] = jnp.where(replaced, HIDDEN_POSITION, place)


def prepare(holds_key, own, partner, cosine, signed_sine, chosen):
    block = pl.BlockSpec((SPAN, HD), lambda step, flag: (step, 0))
    angle = pl.BlockSpec((1, 1, HD), lambda step, flag: (step, 0, 0))
    return pl.pallas_call(
        prepare_kernel,
        out_shape=(
            jax.ShapeDtypeStruct((LENGTH, HD), jnp.bfloat16),
            jax.ShapeDtypeStruct((HD, LENGTH), jnp.bfloat16),
            jax.ShapeDtypeStruct((LENGTH, HD), jnp.int32),
        ),
        grid_spec=pltpu.PrefetchScalarGridSpec(
            num_scalar_prefetch=1,
            grid=(NCHUNK,),
            in_specs=[
                block,
                block,
                angle,
                angle,
                pl.BlockSpec((1, chosen.shape[1]), lambda step, flag: (0, 0)),
            ],
            out_specs=(
                block,
                pl.BlockSpec((HD, SPAN), lambda step, flag: (0, step)),
                block,
            ),
        ),
        cost_estimate=pl.CostEstimate(flops=10**7, bytes_accessed=12 * 2**20, transcendentals=0),
        name="prepare",
    )(holds_key, own, partner, cosine, signed_sine, chosen)


def project_kernel(offsets, token_count, weight_count, done, *refs):
    token_place_ref, weight_place_ref, gain_ref, cosine_ref, sine_ref, old_key_ref, old_value_ref = refs[:7]
    refs = refs[7:]
    token_refs, refs = refs[:token_count], refs[token_count:]
    weight_refs, refs = refs[:weight_count], refs[weight_count:]
    query_ref, key_ref, value_ref, held, weights, total, squares, token_sem, weight_sem = refs
    blocks, slots, width = held.shape
    token_copies = []
    for piece, ref in enumerate(token_refs):
        for part in range(ref.shape[0]):
            number = len(token_copies)
            where = held.at[token_place_ref[number], pl.ds(offsets[piece], ref.shape[1]), :]
            token_copies.append(pltpu.make_async_copy(ref.at[part], where, token_sem.at[number]))
    weight_copies = []
    for piece, ref in enumerate(weight_refs):
        start = pl.multiple_of(weight_place_ref[piece] * width, width)
        where = weights.at[pl.ds(start, ref.shape[0]), :]
        weight_copies.append(pltpu.make_async_copy(ref, where, weight_sem.at[piece]))
    for copy in token_copies + weight_copies:
        copy.start()
    squares[...] = jnp.zeros_like(squares)
    number = 0
    for piece, ref in enumerate(token_refs):
        for _ in range(ref.shape[0]):
            token_copies[number].wait()
            block = token_place_ref[number]
            number += 1

            def add_squares(tile, carry, block=block, offset=offsets[piece]):
                rows = pl.ds(pl.multiple_of(offset + tile * TILE, TILE), TILE)
                hidden = held[block, rows, :].astype(jnp.float32)
                hidden = hidden * hidden
                part = hidden[:, :HD]
                for start in range(HD, width, HD):
                    part = part + hidden[:, start : start + HD]
                squares[rows, :] += part
                return carry

            lax.fori_loop(0, ref.shape[1] // TILE, add_squares, 0)
    mean_square = jnp.sum(squares[...], axis=1, keepdims=True) * (1.0 / (blocks * width))
    squares[...] = jnp.broadcast_to(lax.rsqrt(mean_square + epsilon), squares.shape)
    for copy in weight_copies:
        copy.wait()

    def project_rows(tile, carry):
        rows = pl.ds(pl.multiple_of(tile * ROWS, ROWS), ROWS)
        scale = jnp.concatenate([squares[rows, :]] * (width // HD), axis=1)

        def add_blocks(group, carry):
            normed = []
            for part in range(GROUP):
                block = group * GROUP + part
                hidden = held[block, rows, :].astype(jnp.float32) * scale
                normed.append((hidden * gain_ref[block].astype(jnp.float32)).astype(jnp.bfloat16))
            depth = GROUP * width
            start = pl.multiple_of(group * depth, depth)
            product = jnp.dot(
                jnp.concatenate(normed, axis=1),
                weights[pl.ds(start, depth), :],
                preferred_element_type=jnp.float32,
            )
            total[rows, :] = jnp.where(group == 0, 0.0, total[rows, :]) + product
            return carry

        return lax.fori_loop(0, blocks // GROUP, add_blocks, carry)

    total[...] = jnp.zeros_like(total)
    lax.fori_loop(0, slots // ROWS, project_rows, 0)
    cosine, signed_sine = cosine_ref[...], sine_ref[...]
    for head in range(HEADS):
        part = total[:, head * HD : (head + 1) * HD]
        query_ref[head] = rotate(part, cosine, signed_sine).astype(jnp.bfloat16)
    if done:
        key_ref[:done, :] = old_key_ref[:done, :]
        value_ref[:, :done] = old_value_ref[:, :done]
    key_ref[done : done + slots, :] = rotate(
        total[:, HEADS * HD : (HEADS + 1) * HD], cosine, signed_sine
    ).astype(jnp.bfloat16)
    value_ref[:, done : done + slots] = total[:, (HEADS + 1) * HD :].T.astype(jnp.bfloat16)
    if done + slots < key_ref.shape[0]:
        key_ref[done + slots :, :] = jnp.zeros_like(key_ref[done + slots :, :])
        value_ref[:, done + slots :] = jnp.zeros_like(value_ref[:, done + slots :])


def project(token_pieces, offsets, token_places, gain, cosine, signed_sine, weight_pieces, weight_places, done, old):
    slots = cosine.shape[0]
    width = token_pieces[0].shape[-1]
    blocks = gain.shape[0]
    columns = (HEADS + 2) * HD
    fresh = -(-(done + slots) // KEYS) * KEYS
    whole = pl.BlockSpec(memory_space=pltpu.VMEM)
    remote = pl.BlockSpec(memory_space=pl.ANY)
    scalars = pl.BlockSpec(memory_space=pltpu.SMEM)
    return pl.pallas_call(
        functools.partial(project_kernel, offsets, len(token_pieces), len(weight_pieces), done),
        out_shape=(
            jax.ShapeDtypeStruct((HEADS, slots, HD), jnp.bfloat16),
            jax.ShapeDtypeStruct((fresh, HD), jnp.bfloat16),
            jax.ShapeDtypeStruct((HD, fresh), jnp.bfloat16),
        ),
        in_specs=[scalars, scalars, whole, whole, whole, whole, whole]
        + [remote] * (len(token_pieces) + len(weight_pieces)),
        out_specs=(whole, whole, whole),
        scratch_shapes=[
            pltpu.VMEM((blocks, slots, width), jnp.bfloat16),
            pltpu.VMEM((blocks * width, columns), jnp.bfloat16),
            pltpu.VMEM((slots, columns), jnp.float32),
            pltpu.VMEM((slots, HD), jnp.float32),
            pltpu.SemaphoreType.DMA((token_places.shape[0],)),
            pltpu.SemaphoreType.DMA((len(weight_pieces),)),
        ],
        compiler_params=pltpu.CompilerParams(vmem_limit_bytes=48 * 2**20),
        cost_estimate=pl.CostEstimate(
            flops=4 * slots * blocks * width * columns,
            bytes_accessed=2 * blocks * width * (slots + columns),
            transcendentals=0,
        ),
        name="project",
    )(token_places, weight_places, gain, cosine, signed_sine, *old, *token_pieces, *weight_pieces)


def attend_kernel(
    first,
    blocks_ref,
    query_ref,
    chosen_ref,
    key_ref,
    value_ref,
    place_ref,
    fresh_key_ref,
    fresh_value_ref,
    fresh_place_ref,
    out_ref,
    peak,
    denominator,
    numerator,
    held,
):
    step = pl.program_id(0)
    rows = HEADS * SLOTS
    peak[...] = jnp.full_like(peak, masked_score)
    denominator[...] = jnp.zeros_like(denominator)
    numerator[...] = jnp.zeros_like(numerator)
    queries = query_ref[...].reshape(rows, HD)
    limit = jnp.concatenate([chosen_ref[...]] * HEADS, axis=1)

    def score(keys, block, slot):
        start = pl.multiple_of(block * KEYS, KEYS)
        held[slot] = lax.dot_general(
            keys[pl.ds(start, KEYS), :],
            queries,
            (((1,), (1,)), ((), ())),
            preferred_element_type=jnp.float32,
        )

    def gather(values, places, block, slot):
        start = pl.multiple_of(block * KEYS, KEYS)
        place = jnp.concatenate([places[pl.ds(start, KEYS), :]] * HEADS, axis=1)
        scores = jnp.where(place <= limit, held[slot], masked_score)
        old_peak = peak[...]
        new_peak = jnp.maximum(old_peak, jnp.max(scores, axis=0, keepdims=True))
        rescale = jnp.exp2((old_peak - new_peak) * exponent_scale)
        weights = jnp.exp2((scores - new_peak) * exponent_scale)
        denominator[...] = denominator[...] * rescale + jnp.sum(weights, axis=0, keepdims=True)
        numerator[...] = numerator[...] * rescale + jnp.dot(
            values[:, pl.ds(start, KEYS)],
            weights.astype(jnp.bfloat16),
            preferred_element_type=jnp.float32,
        )
        peak[...] = new_peak

    def walk(keys, values, places, count):
        last = jnp.maximum(count - 1, 0)
        score(keys, 0, 0)

        def pair(turn, carry):
            block = 2 * turn
            score(keys, jnp.minimum(block + 1, last), 1)
            gather(values, places, block, 0)
            score(keys, jnp.minimum(block + 2, last), 0)
            gather(values, places, block + 1, 1)
            return carry

        lax.fori_loop(0, count // 2, pair, 0)

        @pl.when(count % 2 == 1)
        def _():
            gather(values, places, count - 1, 0)

    walk(key_ref, value_ref, place_ref, blocks_ref[step])
    walk(
        fresh_key_ref,
        fresh_value_ref,
        fresh_place_ref,
        ((first + step + 1) * SLOTS + KEYS - 1) // KEYS,
    )
    outcome = jnp.where(limit < LENGTH, numerator[...] / denominator[...], 0.0)
    for head in range(HEADS):
        part = outcome[:, head * SLOTS : (head + 1) * SLOTS]
        out_ref[:, head * HD : (head + 1) * HD] = part.T.astype(jnp.bfloat16)


def attend(first, key_blocks, queries, chosen, keys, values, places, fresh_keys, fresh_values, fresh_places):
    slots = queries.shape[1]
    rows = HEADS * SLOTS

    def still(array):
        return pl.BlockSpec(
            array.shape, lambda step, counts: (0, 0), pipeline_mode=pl.Buffered(1)
        )

    return pl.pallas_call(
        functools.partial(attend_kernel, first),
        out_shape=jax.ShapeDtypeStruct((slots, HEADS * HD), jnp.bfloat16),
        grid_spec=pltpu.PrefetchScalarGridSpec(
            num_scalar_prefetch=1,
            grid=(slots // SLOTS,),
            in_specs=[
                pl.BlockSpec((HEADS, SLOTS, HD), lambda step, counts: (0, step, 0)),
                pl.BlockSpec((1, SLOTS), lambda step, counts: (0, step)),
                still(keys),
                still(values),
                still(places),
                still(fresh_keys),
                still(fresh_values),
                still(fresh_places),
            ],
            out_specs=pl.BlockSpec((SLOTS, HEADS * HD), lambda step, counts: (step, 0)),
            scratch_shapes=[
                pltpu.VMEM((1, rows), jnp.float32),
                pltpu.VMEM((1, rows), jnp.float32),
                pltpu.VMEM((HD, rows), jnp.float32),
                pltpu.VMEM((2, KEYS, rows), jnp.float32),
            ],
        ),
        compiler_params=pltpu.CompilerParams(vmem_limit_bytes=48 * 2**20),
        cost_estimate=pl.CostEstimate(
            flops=slots * HEADS * LENGTH * HD * 2,
            bytes_accessed=12 * 2**20,
            transcendentals=slots * HEADS * LENGTH // 2,
        ),
        name="attend",
    )(key_blocks, queries, chosen, keys, values, places, fresh_keys, fresh_values, fresh_places)


def ring(block, axis, shift):
    half = block.shape[-2] // 2
    behind = lax.ppermute(block, axis, shift(1))
    ahead = lax.ppermute(block, axis, shift(-1))
    far_first = lax.ppermute(behind[..., :half, :], axis, shift(1))
    far_second = lax.ppermute(ahead[..., half:, :], axis, shift(-1))
    return [block, behind, ahead, far_first, far_second]


def shards(tokens, norm_gain, w_query, w_keyval, kv_cache, selected, anchor):
    row_index = lax.axis_index("row")
    col_index = lax.axis_index("col")
    own_x, own_core = row_index // 2, row_index % 2
    holds_key = col_index % 2 == 0
    own_cache = kv_cache[0]
    chosen = selected[0]
    slot_count = chosen.shape[0]
    early = EARLY * SLOTS
    other_keyval = lax.ppermute(w_keyval, "col", flipped(16))
    early_tokens = lax.all_gather(tokens[0, :early], "col", axis=0)
    late_tokens, other_keyval = lax.optimization_barrier((tokens[0, early:], other_keyval))
    late_tokens = lax.all_gather(late_tokens, "col", axis=0)
    other_cache = lax.ppermute(own_cache, "col", flipped(16))

    weights = jnp.concatenate(
        [
            w_query,
            jnp.where(holds_key, w_keyval, other_keyval),
            jnp.where(holds_key, other_keyval, w_keyval),
        ],
        axis=1,
    )
    mine = ring(weights, "row", row_shift)
    theirs = [lax.ppermute(piece, "row", flipped(8)) for piece in mine]
    steps_x = jnp.array([0, 3, 1, 2, 2], jnp.int32)
    second_half = jnp.array([0, 0, 0, 0, 1], jnp.int32)
    source_x = (own_x + steps_x) % 4
    weight_places = jnp.concatenate(
        [
            (source_x * 2 + own_core) * 2 + second_half,
            (source_x * 2 + 1 - own_core) * 2 + second_half,
        ]
    )

    cosine, signed_sine = angles(chosen.astype(jnp.float32), HD)
    span_starts = jnp.arange(NCHUNK, dtype=jnp.int32) * SPAN - anchor[0]
    span_cosine, span_sine = angles(span_starts.astype(jnp.float32), HD)
    keys, values, key_places = prepare(
        holds_key.astype(jnp.int32)[None],
        own_cache,
        other_cache,
        span_cosine[:, None],
        span_sine[:, None],
        chosen[None],
    )
    grouped = chosen.reshape(-1, SLOTS)
    farthest = jnp.max(jnp.where(grouped < LENGTH, grouped, -1), axis=1)
    key_blocks = (farthest + KEYS) // KEYS
    padded = -(-slot_count // KEYS) * KEYS - slot_count
    fresh_places = jnp.broadcast_to(
        jnp.pad(chosen, (0, padded), constant_values=HIDDEN_POSITION)[:, None],
        (slot_count + padded, HD),
    )
    gain = norm_gain.reshape(NCHUNK, 1, -1)
    nothing = (jnp.zeros((16, HD), jnp.bfloat16), jnp.zeros((16, HD), jnp.bfloat16))
    absolute = jnp.arange(NCHUNK, dtype=jnp.int32)
    results = []
    fresh = nothing
    for start, stop, pieces, piece_offsets, piece_places in (
        (0, early, [early_tokens], (0,), absolute),
        (early, slot_count, [late_tokens], (0,), absolute),
    ):
        queries, *fresh = project(
            pieces,
            piece_offsets,
            piece_places,
            gain,
            cosine[start:stop],
            signed_sine[start:stop],
            mine + theirs,
            weight_places,
            start,
            fresh,
        )
        results.append(
            attend(
                start // SLOTS,
                key_blocks[start // SLOTS : stop // SLOTS],
                queries,
                chosen[None, start:stop],
                keys,
                values,
                key_places,
                *fresh,
                fresh_places,
            )
        )
    return jnp.concatenate(results, axis=0)[None]


def solution(mesh):
    in_specs = (
        P("row", None, "col"),
        P(),
        P("row", "col"),
        P("row", "col"),
        P("row", None, "col"),
        P("row", None),
        P("row", None),
    )
    out_specs = P("row", None, "col")
    return jax.shard_map(shards, mesh=mesh, in_specs=in_specs, out_specs=out_specs, check_vma=False)
```

```python
import functools
import math

import jax
import jax.numpy as jnp
from jax import lax
from jax.experimental import pallas as pl
from jax.experimental.pallas import tpu as pltpu
from jax.sharding import PartitionSpec as P

HD = 128
SPAN = 512
NCHUNK = 16
LENGTH = SPAN * NCHUNK
HEADS = 4
KEYS = 512
SLOTS = 128
HIDDEN_POSITION = 4 * LENGTH
EARLY = 6
NEAR = 12
TILE = 64
ROWS = 384
GROUP = 4

rope_base = 500000.0
epsilon = 1e-05
masked_score = -1e30
exponent_scale = HD ** (-0.5) * math.log2(math.e)


def col_shift(dy, dz):
    return [(4 * y + z, 4 * ((y + dy) % 4) + (z + dz) % 4) for y in range(4) for z in range(4)]


def row_shift(dx):
    return [(2 * x + core, 2 * ((x + dx) % 4) + core) for x in range(4) for core in range(2)]


def flipped(count):
    return [(place, place ^ 1) for place in range(count)]


def angles(positions, width):
    half_width = width // 2
    exponents = jnp.arange(half_width, dtype=jnp.float32) * (-2.0 / width)
    frequency = jnp.exp(exponents * math.log(rope_base))
    phases = positions[..., None] * frequency
    cosine, sine_part = jnp.cos(phases), jnp.sin(phases)
    return (
        jnp.concatenate([cosine, cosine], axis=-1),
        jnp.concatenate([-sine_part, sine_part], axis=-1),
    )


def rotate(vectors, cosine, signed_sine):
    return vectors * cosine + pltpu.roll(vectors, HD // 2, 1) * signed_sine


def prepare_kernel(first, holds_key_ref, own_ref, partner_ref, cosine_ref, sine_ref, chosen_ref, *refs):
    key_ref, value_ref, place_ref = refs[-3:]
    step = first + pl.program_id(0)
    holds_key = holds_key_ref[0] == 1
    own = own_ref[...]
    partner = partner_ref[...]
    stored_key = jnp.where(holds_key, own, partner).astype(jnp.float32)
    stored_value = jnp.where(holds_key, partner, own).astype(jnp.float32)
    key_ref[...] = rotate(stored_key, cosine_ref[0], sine_ref[0]).astype(jnp.bfloat16)
    value_ref[...] = stored_value.T.astype(jnp.bfloat16)
    place = step * SPAN + lax.broadcasted_iota(jnp.int32, (SPAN, HD), 0)
    seen = jnp.zeros((SPAN, HD), jnp.int32)
    for start in range(0, chosen_ref.shape[1], HD):
        seen = jnp.where(place == chosen_ref[0:1, start : start + HD], 1, seen)
    replaced = jnp.max(seen, axis=1, keepdims=True) > 0
    place_ref[...] = jnp.where(replaced, HIDDEN_POSITION, place)


def prepare(first, holds_key, own, partner, cosine, signed_sine, chosen, earlier):
    block = pl.BlockSpec((SPAN, HD), lambda step, flag: (first + step, 0))
    angle = pl.BlockSpec((1, 1, HD), lambda step, flag: (first + step, 0, 0))
    return pl.pallas_call(
        functools.partial(prepare_kernel, first),
        out_shape=(
            jax.ShapeDtypeStruct((LENGTH, HD), jnp.bfloat16),
            jax.ShapeDtypeStruct((HD, LENGTH), jnp.bfloat16),
            jax.ShapeDtypeStruct((LENGTH, HD), jnp.int32),
        ),
        grid_spec=pltpu.PrefetchScalarGridSpec(
            num_scalar_prefetch=1,
            grid=(partner.shape[0] // SPAN,),
            in_specs=[
                block,
                pl.BlockSpec((SPAN, HD), lambda step, flag: (step, 0)),
                angle,
                angle,
                pl.BlockSpec((1, chosen.shape[1]), lambda step, flag: (0, 0)),
            ]
            + [pl.BlockSpec(memory_space=pl.ANY)] * len(earlier),
            out_specs=(
                block,
                pl.BlockSpec((HD, SPAN), lambda step, flag: (0, first + step)),
                block,
            ),
        ),
        input_output_aliases={6 + number: number for number in range(len(earlier))},
        cost_estimate=pl.CostEstimate(flops=10**7, bytes_accessed=6 * 2**20, transcendentals=0),
        name="prepare",
    )(holds_key, own, partner, cosine, signed_sine, chosen, *earlier)


def project_kernel(offsets, token_count, weight_count, done, *refs):
    token_place_ref, weight_place_ref, gain_ref, cosine_ref, sine_ref, old_key_ref, old_value_ref = refs[:7]
    refs = refs[7:]
    token_refs, refs = refs[:token_count], refs[token_count:]
    weight_refs, refs = refs[:weight_count], refs[weight_count:]
    query_ref, key_ref, value_ref, held, weights, total, squares, token_sem, weight_sem = refs
    blocks, slots, width = held.shape
    token_copies = []
    for piece, ref in enumerate(token_refs):
        for part in range(ref.shape[0]):
            number = len(token_copies)
            where = held.at[token_place_ref[number], pl.ds(offsets[piece], ref.shape[1]), :]
            token_copies.append(pltpu.make_async_copy(ref.at[part], where, token_sem.at[number]))
    weight_copies = []
    for piece, ref in enumerate(weight_refs):
        start = pl.multiple_of(weight_place_ref[piece] * width, width)
        where = weights.at[pl.ds(start, ref.shape[0]), :]
        weight_copies.append(pltpu.make_async_copy(ref, where, weight_sem.at[piece]))
    for copy in token_copies + weight_copies:
        copy.start()
    squares[...] = jnp.zeros_like(squares)
    number = 0
    for piece, ref in enumerate(token_refs):
        for _ in range(ref.shape[0]):
            token_copies[number].wait()
            block = token_place_ref[number]
            number += 1

            def add_squares(tile, carry, block=block, offset=offsets[piece]):
                rows = pl.ds(pl.multiple_of(offset + tile * TILE, TILE), TILE)
                hidden = held[block, rows, :].astype(jnp.float32)
                hidden = hidden * hidden
                part = hidden[:, :HD]
                for start in range(HD, width, HD):
                    part = part + hidden[:, start : start + HD]
                squares[rows, :] += part
                return carry

            lax.fori_loop(0, ref.shape[1] // TILE, add_squares, 0)
    mean_square = jnp.sum(squares[...], axis=1, keepdims=True) * (1.0 / (blocks * width))
    squares[...] = jnp.broadcast_to(lax.rsqrt(mean_square + epsilon), squares.shape)
    for copy in weight_copies:
        copy.wait()

    height = slots // max(1, slots // ROWS)

    def project_rows(tile, carry):
        rows = pl.ds(pl.multiple_of(tile * height, height), height)
        scale = jnp.concatenate([squares[rows, :]] * (width // HD), axis=1)

        def add_blocks(group, carry):
            normed = []
            for part in range(GROUP):
                block = group * GROUP + part
                hidden = held[block, rows, :].astype(jnp.float32) * scale
                normed.append((hidden * gain_ref[block].astype(jnp.float32)).astype(jnp.bfloat16))
            depth = GROUP * width
            start = pl.multiple_of(group * depth, depth)
            product = jnp.dot(
                jnp.concatenate(normed, axis=1),
                weights[pl.ds(start, depth), :],
                preferred_element_type=jnp.float32,
            )
            total[rows, :] = jnp.where(group == 0, 0.0, total[rows, :]) + product
            return carry

        return lax.fori_loop(0, blocks // GROUP, add_blocks, carry)

    total[...] = jnp.zeros_like(total)
    lax.fori_loop(0, slots // height, project_rows, 0)
    cosine, signed_sine = cosine_ref[...], sine_ref[...]
    for head in range(HEADS):
        part = total[:, head * HD : (head + 1) * HD]
        query_ref[head] = rotate(part, cosine, signed_sine).astype(jnp.bfloat16)
    if done:
        key_ref[:done, :] = old_key_ref[:done, :]
        value_ref[:, :done] = old_value_ref[:, :done]
    key_ref[done : done + slots, :] = rotate(
        total[:, HEADS * HD : (HEADS + 1) * HD], cosine, signed_sine
    ).astype(jnp.bfloat16)
    value_ref[:, done : done + slots] = total[:, (HEADS + 1) * HD :].T.astype(jnp.bfloat16)
    if done + slots < key_ref.shape[0]:
        key_ref[done + slots :, :] = jnp.zeros_like(key_ref[done + slots :, :])
        value_ref[:, done + slots :] = jnp.zeros_like(value_ref[:, done + slots :])


def project(token_pieces, offsets, token_places, gain, cosine, signed_sine, weight_pieces, weight_places, done, old):
    slots = cosine.shape[0]
    width = token_pieces[0].shape[-1]
    blocks = gain.shape[0]
    columns = (HEADS + 2) * HD
    fresh = -(-(done + slots) // KEYS) * KEYS
    whole = pl.BlockSpec(memory_space=pltpu.VMEM)
    remote = pl.BlockSpec(memory_space=pl.ANY)
    scalars = pl.BlockSpec(memory_space=pltpu.SMEM)
    return pl.pallas_call(
        functools.partial(project_kernel, offsets, len(token_pieces), len(weight_pieces), done),
        out_shape=(
            jax.ShapeDtypeStruct((HEADS, slots, HD), jnp.bfloat16),
            jax.ShapeDtypeStruct((fresh, HD), jnp.bfloat16),
            jax.ShapeDtypeStruct((HD, fresh), jnp.bfloat16),
        ),
        in_specs=[scalars, scalars, whole, whole, whole, whole, whole]
        + [remote] * (len(token_pieces) + len(weight_pieces)),
        out_specs=(whole, whole, whole),
        scratch_shapes=[
            pltpu.VMEM((blocks, slots, width), jnp.bfloat16),
            pltpu.VMEM((blocks * width, columns), jnp.bfloat16),
            pltpu.VMEM((slots, columns), jnp.float32),
            pltpu.VMEM((slots, HD), jnp.float32),
            pltpu.SemaphoreType.DMA((token_places.shape[0],)),
            pltpu.SemaphoreType.DMA((len(weight_pieces),)),
        ],
        compiler_params=pltpu.CompilerParams(vmem_limit_bytes=48 * 2**20),
        cost_estimate=pl.CostEstimate(
            flops=4 * slots * blocks * width * columns,
            bytes_accessed=2 * blocks * width * (slots + columns),
            transcendentals=0,
        ),
        name="project",
    )(token_places, weight_places, gain, cosine, signed_sine, *old, *token_pieces, *weight_pieces)


def attend_kernel(
    first,
    blocks_ref,
    query_ref,
    chosen_ref,
    key_ref,
    value_ref,
    place_ref,
    fresh_key_ref,
    fresh_value_ref,
    fresh_place_ref,
    out_ref,
    peak,
    denominator,
    numerator,
    held,
):
    step = pl.program_id(0)
    rows = HEADS * SLOTS
    peak[...] = jnp.full_like(peak, masked_score)
    denominator[...] = jnp.zeros_like(denominator)
    numerator[...] = jnp.zeros_like(numerator)
    queries = query_ref[...].reshape(rows, HD)
    limit = jnp.concatenate([chosen_ref[...]] * HEADS, axis=1)

    def score(keys, block, slot):
        start = pl.multiple_of(block * KEYS, KEYS)
        held[slot] = lax.dot_general(
            keys[pl.ds(start, KEYS), :],
            queries,
            (((1,), (1,)), ((), ())),
            preferred_element_type=jnp.float32,
        )

    def gather(values, places, block, slot):
        start = pl.multiple_of(block * KEYS, KEYS)
        place = jnp.concatenate([places[pl.ds(start, KEYS), :]] * HEADS, axis=1)
        scores = jnp.where(place <= limit, held[slot], masked_score)
        old_peak = peak[...]
        new_peak = jnp.maximum(old_peak, jnp.max(scores, axis=0, keepdims=True))
        rescale = jnp.exp2((old_peak - new_peak) * exponent_scale)
        weights = jnp.exp2((scores - new_peak) * exponent_scale)
        denominator[...] = denominator[...] * rescale + jnp.sum(weights, axis=0, keepdims=True)
        numerator[...] = numerator[...] * rescale + jnp.dot(
            values[:, pl.ds(start, KEYS)],
            weights.astype(jnp.bfloat16),
            preferred_element_type=jnp.float32,
        )
        peak[...] = new_peak

    def walk(keys, values, places, count):
        last = jnp.maximum(count - 1, 0)
        score(keys, 0, 0)

        def pair(turn, carry):
            block = 2 * turn
            score(keys, jnp.minimum(block + 1, last), 1)
            gather(values, places, block, 0)
            score(keys, jnp.minimum(block + 2, last), 0)
            gather(values, places, block + 1, 1)
            return carry

        lax.fori_loop(0, count // 2, pair, 0)

        @pl.when(count % 2 == 1)
        def _():
            gather(values, places, count - 1, 0)

    walk(key_ref, value_ref, place_ref, blocks_ref[step])
    walk(
        fresh_key_ref,
        fresh_value_ref,
        fresh_place_ref,
        ((first + step + 1) * SLOTS + KEYS - 1) // KEYS,
    )
    outcome = jnp.where(limit < LENGTH, numerator[...] / denominator[...], 0.0)
    for head in range(HEADS):
        part = outcome[:, head * SLOTS : (head + 1) * SLOTS]
        out_ref[:, head * HD : (head + 1) * HD] = part.T.astype(jnp.bfloat16)


def attend(first, key_blocks, queries, chosen, keys, values, places, fresh_keys, fresh_values, fresh_places):
    slots = queries.shape[1]
    rows = HEADS * SLOTS

    def still(array):
        return pl.BlockSpec(
            array.shape, lambda step, counts: (0, 0), pipeline_mode=pl.Buffered(1)
        )

    return pl.pallas_call(
        functools.partial(attend_kernel, first),
        out_shape=jax.ShapeDtypeStruct((slots, HEADS * HD), jnp.bfloat16),
        grid_spec=pltpu.PrefetchScalarGridSpec(
            num_scalar_prefetch=1,
            grid=(slots // SLOTS,),
            in_specs=[
                pl.BlockSpec((HEADS, SLOTS, HD), lambda step, counts: (0, step, 0)),
                pl.BlockSpec((1, SLOTS), lambda step, counts: (0, step)),
                still(keys),
                still(values),
                still(places),
                still(fresh_keys),
                still(fresh_values),
                still(fresh_places),
            ],
            out_specs=pl.BlockSpec((SLOTS, HEADS * HD), lambda step, counts: (step, 0)),
            scratch_shapes=[
                pltpu.VMEM((1, rows), jnp.float32),
                pltpu.VMEM((1, rows), jnp.float32),
                pltpu.VMEM((HD, rows), jnp.float32),
                pltpu.VMEM((2, KEYS, rows), jnp.float32),
            ],
        ),
        compiler_params=pltpu.CompilerParams(vmem_limit_bytes=48 * 2**20),
        cost_estimate=pl.CostEstimate(
            flops=slots * HEADS * LENGTH * HD * 2,
            bytes_accessed=12 * 2**20,
            transcendentals=slots * HEADS * LENGTH // 2,
        ),
        name="attend",
    )(key_blocks, queries, chosen, keys, values, places, fresh_keys, fresh_values, fresh_places)


def ring(block, axis, shift):
    half = block.shape[-2] // 2
    behind = lax.ppermute(block, axis, shift(1))
    ahead = lax.ppermute(block, axis, shift(-1))
    far_first = lax.ppermute(behind[..., :half, :], axis, shift(1))
    far_second = lax.ppermute(ahead[..., half:, :], axis, shift(-1))
    return [block, behind, ahead, far_first, far_second]


def shards(tokens, norm_gain, w_query, w_keyval, kv_cache, selected, anchor):
    row_index = lax.axis_index("row")
    col_index = lax.axis_index("col")
    own_x, own_core = row_index // 2, row_index % 2
    holds_key = col_index % 2 == 0
    own_cache = kv_cache[0]
    chosen = selected[0]
    slot_count = chosen.shape[0]
    early = EARLY * SLOTS
    middle = NEAR * SPAN
    near_cache = lax.ppermute(own_cache[:middle], "col", flipped(16))
    early_tokens = lax.all_gather(tokens[0, :early], "col", axis=0)
    other_keyval = lax.ppermute(w_keyval, "col", flipped(16))
    late_tokens, other_keyval = lax.optimization_barrier((tokens[0, early:], other_keyval))
    late_tokens = lax.all_gather(late_tokens, "col", axis=0)
    far_cache, early_tokens = lax.optimization_barrier((own_cache[middle:], early_tokens))
    far_cache = lax.ppermute(far_cache, "col", flipped(16))

    weights = jnp.concatenate(
        [
            w_query,
            jnp.where(holds_key, w_keyval, other_keyval),
            jnp.where(holds_key, other_keyval, w_keyval),
        ],
        axis=1,
    )
    mine = ring(weights, "row", row_shift)
    theirs = [lax.ppermute(piece, "row", flipped(8)) for piece in mine]
    steps_x = jnp.array([0, 3, 1, 2, 2], jnp.int32)
    second_half = jnp.array([0, 0, 0, 0, 1], jnp.int32)
    source_x = (own_x + steps_x) % 4
    weight_places = jnp.concatenate(
        [
            (source_x * 2 + own_core) * 2 + second_half,
            (source_x * 2 + 1 - own_core) * 2 + second_half,
        ]
    )

    cosine, signed_sine = angles(chosen.astype(jnp.float32), HD)
    span_starts = jnp.arange(NCHUNK, dtype=jnp.int32) * SPAN - anchor[0]
    span_cosine, span_sine = angles(span_starts.astype(jnp.float32), HD)
    prepared = ()
    for first_span, partner in ((0, near_cache), (NEAR, far_cache)):
        prepared = prepare(
            first_span,
            holds_key.astype(jnp.int32)[None],
            own_cache,
            partner,
            span_cosine[:, None],
            span_sine[:, None],
            chosen[None],
            prepared,
        )
    keys, values, key_places = prepared
    grouped = chosen.reshape(-1, SLOTS)
    farthest = jnp.max(jnp.where(grouped < LENGTH, grouped, -1), axis=1)
    key_blocks = (farthest + KEYS) // KEYS
    padded = -(-slot_count // KEYS) * KEYS - slot_count
    fresh_places = jnp.broadcast_to(
        jnp.pad(chosen, (0, padded), constant_values=HIDDEN_POSITION)[:, None],
        (slot_count + padded, HD),
    )
    gain = norm_gain.reshape(NCHUNK, 1, -1)
    nothing = (jnp.zeros((16, HD), jnp.bfloat16), jnp.zeros((16, HD), jnp.bfloat16))
    absolute = jnp.arange(NCHUNK, dtype=jnp.int32)
    results = []
    fresh = nothing
    for start, stop, pieces, piece_offsets, piece_places in (
        (0, early, [early_tokens], (0,), absolute),
        (early, slot_count, [late_tokens], (0,), absolute),
    ):
        if results:
            results[0], pieces = lax.optimization_barrier((results[0], pieces))
        queries, *fresh = project(
            pieces,
            piece_offsets,
            piece_places,
            gain,
            cosine[start:stop],
            signed_sine[start:stop],
            mine + theirs,
            weight_places,
            start,
            fresh,
        )
        results.append(
            attend(
                start // SLOTS,
                key_blocks[start // SLOTS : stop // SLOTS],
                queries,
                chosen[None, start:stop],
                keys,
                values,
                key_places,
                *fresh,
                fresh_places,
            )
        )
    return jnp.concatenate(results, axis=0)[None]


def solution(mesh):
    in_specs = (
        P("row", None, "col"),
        P(),
        P("row", "col"),
        P("row", "col"),
        P("row", None, "col"),
        P("row", None),
        P("row", None),
    )
    out_specs = P("row", None, "col")
    return jax.shard_map(shards, mesh=mesh, in_specs=in_specs, out_specs=out_specs, check_vma=False)
```

```python
import functools
import math

import jax
import jax.numpy as jnp
from jax import lax
from jax.experimental import pallas as pl
from jax.experimental.pallas import tpu as pltpu
from jax.sharding import PartitionSpec as P

HD = 128
SPAN = 512
NCHUNK = 16
LENGTH = SPAN * NCHUNK
HEADS = 4
KEYS = 512
SLOTS = 128
HIDDEN_POSITION = 4 * LENGTH
EARLY = 6
NEAR = 12
TILE = 64
ROWS = 384
GROUP = 4

rope_base = 500000.0
epsilon = 1e-05
masked_score = -1e30
exponent_scale = HD ** (-0.5) * math.log2(math.e)


def col_shift(dy, dz):
    return [(4 * y + z, 4 * ((y + dy) % 4) + (z + dz) % 4) for y in range(4) for z in range(4)]


def row_shift(dx):
    return [(2 * x + core, 2 * ((x + dx) % 4) + core) for x in range(4) for core in range(2)]


def flipped(count):
    return [(place, place ^ 1) for place in range(count)]


def angles(positions, width):
    half_width = width // 2
    exponents = jnp.arange(half_width, dtype=jnp.float32) * (-2.0 / width)
    frequency = jnp.exp(exponents * math.log(rope_base))
    phases = positions[..., None] * frequency
    cosine, sine_part = jnp.cos(phases), jnp.sin(phases)
    return (
        jnp.concatenate([cosine, cosine], axis=-1),
        jnp.concatenate([-sine_part, sine_part], axis=-1),
    )


def rotate(vectors, cosine, signed_sine):
    return vectors * cosine + pltpu.roll(vectors, HD // 2, 1) * signed_sine


def prepare_kernel(holds_key_ref, own_ref, partner_ref, cosine_ref, sine_ref, *refs):
    key_ref, value_ref = refs[-2:]
    holds_key = holds_key_ref[0] == 1
    own = own_ref[...]
    partner = partner_ref[...]
    stored_key = jnp.where(holds_key, own, partner).astype(jnp.float32)
    stored_value = jnp.where(holds_key, partner, own).astype(jnp.float32)
    key_ref[...] = rotate(stored_key, cosine_ref[0], sine_ref[0]).astype(jnp.bfloat16)
    value_ref[...] = stored_value.T.astype(jnp.bfloat16)


def mark_kernel(chosen_ref, place_ref):
    step = pl.program_id(0)

    @pl.when(step < NCHUNK)
    def _():
        place = step * SPAN + lax.broadcasted_iota(jnp.int32, (SPAN, HD), 0)
        seen = jnp.zeros((SPAN, HD), jnp.int32)
        for start in range(0, chosen_ref.shape[1], HD):
            seen = jnp.where(place == chosen_ref[0:1, start : start + HD], 1, seen)
        replaced = jnp.max(seen, axis=1, keepdims=True) > 0
        place_ref[...] = jnp.where(replaced, HIDDEN_POSITION, place)

    @pl.when(step >= NCHUNK)
    def _():
        for part in range(0, SPAN, HD):
            start = pl.multiple_of((step - NCHUNK) * SPAN + part, HD)
            fresh = jnp.broadcast_to(chosen_ref[0:1, pl.ds(start, HD)], (HD, HD))
            place_ref[part : part + HD, :] = fresh.astype(jnp.float32).T.astype(jnp.int32)


def mark(chosen):
    total = LENGTH + chosen.shape[1]
    return pl.pallas_call(
        mark_kernel,
        out_shape=jax.ShapeDtypeStruct((total, HD), jnp.int32),
        grid=(total // SPAN,),
        in_specs=[pl.BlockSpec((1, chosen.shape[1]), lambda step: (0, 0))],
        out_specs=pl.BlockSpec((SPAN, HD), lambda step: (step, 0)),
        cost_estimate=pl.CostEstimate(flops=10**7, bytes_accessed=5 * 2**20, transcendentals=0),
        name="mark",
    )(chosen)


def prepare(first, holds_key, own, partner, cosine, signed_sine, earlier):
    block = pl.BlockSpec((SPAN, HD), lambda step, flag: (first + step, 0))
    angle = pl.BlockSpec((1, 1, HD), lambda step, flag: (first + step, 0, 0))
    return pl.pallas_call(
        prepare_kernel,
        out_shape=(
            jax.ShapeDtypeStruct((LENGTH, HD), jnp.bfloat16),
            jax.ShapeDtypeStruct((HD, LENGTH), jnp.bfloat16),
        ),
        grid_spec=pltpu.PrefetchScalarGridSpec(
            num_scalar_prefetch=1,
            grid=(partner.shape[0] // SPAN,),
            in_specs=[
                block,
                pl.BlockSpec((SPAN, HD), lambda step, flag: (step, 0)),
                angle,
                angle,
            ]
            + [pl.BlockSpec(memory_space=pl.ANY)] * len(earlier),
            out_specs=(
                block,
                pl.BlockSpec((HD, SPAN), lambda step, flag: (0, first + step)),
            ),
        ),
        input_output_aliases={5 + number: number for number in range(len(earlier))},
        cost_estimate=pl.CostEstimate(flops=10**7, bytes_accessed=6 * 2**20, transcendentals=0),
        name="prepare",
    )(holds_key, own, partner, cosine, signed_sine, *earlier)


def project_kernel(offsets, token_count, weight_count, done, *refs):
    weight_place_ref, gain_ref, cosine_ref, sine_ref = refs[:4]
    refs = refs[4:]
    token_refs, refs = refs[:token_count], refs[token_count:]
    weight_refs, refs = refs[:weight_count], refs[weight_count:]
    query_ref, key_ref, value_ref, held, weights, total, squares, token_sem, weight_sem = refs
    blocks, slots, width = held.shape
    token_copies = []
    for piece, ref in enumerate(token_refs):
        for part in range(ref.shape[0]):
            number = len(token_copies)
            where = held.at[part, pl.ds(offsets[piece], ref.shape[1]), :]
            token_copies.append(pltpu.make_async_copy(ref.at[part], where, token_sem.at[number]))
    weight_copies = []
    for piece, ref in enumerate(weight_refs):
        start = pl.multiple_of(weight_place_ref[piece] * width, width)
        where = weights.at[pl.ds(start, ref.shape[0]), :]
        weight_copies.append(pltpu.make_async_copy(ref, where, weight_sem.at[piece]))
    for copy in token_copies + weight_copies:
        copy.start()
    squares[...] = jnp.zeros_like(squares)
    number = 0
    for piece, ref in enumerate(token_refs):
        for block in range(ref.shape[0]):
            token_copies[number].wait()
            number += 1

            def add_squares(tile, carry, block=block, offset=offsets[piece]):
                rows = pl.ds(pl.multiple_of(offset + tile * TILE, TILE), TILE)
                hidden = held[block, rows, :].astype(jnp.float32)
                hidden = hidden * hidden
                part = hidden[:, :HD]
                for start in range(HD, width, HD):
                    part = part + hidden[:, start : start + HD]
                squares[rows, :] += part
                return carry

            lax.fori_loop(0, ref.shape[1] // TILE, add_squares, 0)
    mean_square = jnp.sum(squares[...], axis=1, keepdims=True) * (1.0 / (blocks * width))
    squares[...] = jnp.broadcast_to(lax.rsqrt(mean_square + epsilon), squares.shape)
    for copy in weight_copies:
        copy.wait()

    height = slots // max(1, slots // ROWS)

    def project_rows(tile, carry):
        rows = pl.ds(pl.multiple_of(tile * height, height), height)
        scale = jnp.concatenate([squares[rows, :]] * (width // HD), axis=1)

        def add_blocks(group, carry):
            normed = []
            for part in range(GROUP):
                block = group * GROUP + part
                hidden = held[block, rows, :].astype(jnp.float32) * scale
                normed.append((hidden * gain_ref[block].astype(jnp.float32)).astype(jnp.bfloat16))
            depth = GROUP * width
            start = pl.multiple_of(group * depth, depth)
            product = jnp.dot(
                jnp.concatenate(normed, axis=1),
                weights[pl.ds(start, depth), :],
                preferred_element_type=jnp.float32,
            )
            total[rows, :] = jnp.where(group == 0, 0.0, total[rows, :]) + product
            return carry

        return lax.fori_loop(0, blocks // GROUP, add_blocks, carry)

    total[...] = jnp.zeros_like(total)
    lax.fori_loop(0, slots // height, project_rows, 0)
    cosine, signed_sine = cosine_ref[...], sine_ref[...]
    for head in range(HEADS):
        part = total[:, head * HD : (head + 1) * HD]
        query_ref[head] = rotate(part, cosine, signed_sine).astype(jnp.bfloat16)
    key_ref[done : done + slots, :] = rotate(
        total[:, HEADS * HD : (HEADS + 1) * HD], cosine, signed_sine
    ).astype(jnp.bfloat16)
    value_ref[:, done : done + slots] = total[:, (HEADS + 1) * HD :].T.astype(jnp.bfloat16)
    if done + slots < key_ref.shape[0]:
        key_ref[done + slots :, :] = jnp.zeros_like(key_ref[done + slots :, :])
        value_ref[:, done + slots :] = jnp.zeros_like(value_ref[:, done + slots :])


def project(token_pieces, offsets, gain, cosine, signed_sine, weight_pieces, weight_places, done):
    slots = cosine.shape[0]
    width = token_pieces[0].shape[-1]
    blocks = gain.shape[0]
    columns = (HEADS + 2) * HD
    fresh = -(-(done + slots) // KEYS) * KEYS
    whole = pl.BlockSpec(memory_space=pltpu.VMEM)
    remote = pl.BlockSpec(memory_space=pl.ANY)
    scalars = pl.BlockSpec(memory_space=pltpu.SMEM)
    return pl.pallas_call(
        functools.partial(project_kernel, offsets, len(token_pieces), len(weight_pieces), done),
        out_shape=(
            jax.ShapeDtypeStruct((HEADS, slots, HD), jnp.bfloat16),
            jax.ShapeDtypeStruct((fresh, HD), jnp.bfloat16),
            jax.ShapeDtypeStruct((HD, fresh), jnp.bfloat16),
        ),
        in_specs=[scalars, whole, whole, whole]
        + [remote] * (len(token_pieces) + len(weight_pieces)),
        out_specs=(whole, whole, whole),
        scratch_shapes=[
            pltpu.VMEM((blocks, slots, width), jnp.bfloat16),
            pltpu.VMEM((blocks * width, columns), jnp.bfloat16),
            pltpu.VMEM((slots, columns), jnp.float32),
            pltpu.VMEM((slots, HD), jnp.float32),
            pltpu.SemaphoreType.DMA((blocks * len(token_pieces),)),
            pltpu.SemaphoreType.DMA((len(weight_pieces),)),
        ],
        compiler_params=pltpu.CompilerParams(vmem_limit_bytes=48 * 2**20),
        cost_estimate=pl.CostEstimate(
            flops=4 * slots * blocks * width * columns,
            bytes_accessed=2 * blocks * width * (slots + columns),
            transcendentals=0,
        ),
        name="project",
    )(weight_places, gain, cosine, signed_sine, *token_pieces, *weight_pieces)


def attend_slots(
    asked, chosen, stored, slots_seen, keys, values, places, out_ref, peak, denominator, numerator, score_slots
):
    limit = jnp.concatenate([chosen] * HEADS, axis=1)
    peak[...] = jnp.full_like(peak, masked_score)
    denominator[...] = jnp.zeros_like(denominator)
    numerator[...] = jnp.zeros_like(numerator)
    count = stored + (slots_seen + KEYS - 1) // KEYS

    def start_of(block):
        block = jnp.minimum(block, count - 1)
        block = jnp.where(block < stored, block, block - stored + LENGTH // KEYS)
        return pl.multiple_of(block * KEYS, KEYS)

    def score(block, slot):
        score_slots[slot] = lax.dot_general(
            keys[pl.ds(start_of(block), KEYS), :],
            asked,
            (((1,), (1,)), ((), ())),
            preferred_element_type=jnp.float32,
        )

    def gather(block, slot):
        start = start_of(block)
        place = jnp.concatenate([places[pl.ds(start, KEYS), :]] * HEADS, axis=1)
        scores = jnp.where(place <= limit, score_slots[slot], masked_score)
        old_peak = peak[...]
        new_peak = jnp.maximum(old_peak, jnp.max(scores, axis=0, keepdims=True))
        rescale = jnp.exp2((old_peak - new_peak) * exponent_scale)
        exponentials = jnp.exp2((scores - new_peak) * exponent_scale)
        denominator[...] = denominator[...] * rescale + jnp.sum(
            exponentials, axis=0, keepdims=True
        )
        numerator[...] = numerator[...] * rescale + jnp.dot(
            values[:, pl.ds(start, KEYS)],
            exponentials.astype(jnp.bfloat16),
            preferred_element_type=jnp.float32,
        )
        peak[...] = new_peak

    score(0, 0)

    def pair(turn, carry):
        block = 2 * turn
        score(block + 1, 1)
        gather(block, 0)
        score(block + 2, 0)
        gather(block + 1, 1)
        return carry

    lax.fori_loop(0, count // 2, pair, 0)

    @pl.when(count % 2 == 1)
    def _():
        gather(count - 1, 0)

    outcome = jnp.where(limit < LENGTH, numerator[...] / denominator[...], 0.0)
    for head in range(HEADS):
        part = outcome[:, head * SLOTS : (head + 1) * SLOTS]
        out_ref[:, head * HD : (head + 1) * HD] = part.T.astype(jnp.bfloat16)


def attend_kernel(first, blocks_ref, query_ref, chosen_ref, *refs):
    stored_refs, (out_ref, *scratch) = refs[:5], refs[-9:]
    keys, values, places, peak, denominator, numerator, score_slots, sem = scratch
    step = pl.program_id(0)
    fresh = stored_refs[3].shape[0]

    @pl.when(step == 0)
    def _():
        old, new = pl.ds(0, LENGTH), pl.ds(LENGTH, fresh)
        wheres = (keys.at[old, :], values.at[:, old], places, keys.at[new, :], values.at[:, new])
        held_places = stored_refs[2].at[pl.ds(0, LENGTH + fresh), :]
        sources = (*stored_refs[:2], held_places, *stored_refs[3:])
        copies = [
            pltpu.make_async_copy(source, where, sem.at[number])
            for number, (source, where) in enumerate(zip(sources, wheres))
        ]
        for copy in copies:
            copy.start()
        for copy in copies:
            copy.wait()

    attend_slots(
        query_ref[...].reshape(HEADS * SLOTS, HD), chosen_ref[...], blocks_ref[step],
        (first + step + 1) * SLOTS,
        keys, values, places, out_ref, peak, denominator, numerator, score_slots,
    )


def attend(first, key_blocks, queries, chosen, stored, total_slots):
    slots = queries.shape[1]
    rows = HEADS * SLOTS
    length = LENGTH + stored[3].shape[0]
    return pl.pallas_call(
        functools.partial(attend_kernel, first),
        out_shape=jax.ShapeDtypeStruct((total_slots, HEADS * HD), jnp.bfloat16),
        grid_spec=pltpu.PrefetchScalarGridSpec(
            num_scalar_prefetch=1,
            grid=(slots // SLOTS,),
            in_specs=[
                pl.BlockSpec((HEADS, SLOTS, HD), lambda step, counts: (0, step, 0)),
                pl.BlockSpec((1, SLOTS), lambda step, counts: (0, step)),
            ]
            + [pl.BlockSpec(memory_space=pl.ANY)] * 5,
            out_specs=pl.BlockSpec((SLOTS, HEADS * HD), lambda step, counts: (first + step, 0)),
            scratch_shapes=[
                pltpu.VMEM((length, HD), jnp.bfloat16),
                pltpu.VMEM((HD, length), jnp.bfloat16),
                pltpu.VMEM((length, HD), jnp.int32),
                pltpu.VMEM((1, rows), jnp.float32),
                pltpu.VMEM((1, rows), jnp.float32),
                pltpu.VMEM((HD, rows), jnp.float32),
                pltpu.VMEM((2, KEYS, rows), jnp.float32),
                pltpu.SemaphoreType.DMA((5,)),
            ],
        ),
        compiler_params=pltpu.CompilerParams(vmem_limit_bytes=56 * 2**20),
        cost_estimate=pl.CostEstimate(
            flops=slots * HEADS * LENGTH * HD * 2,
            bytes_accessed=12 * 2**20,
            transcendentals=slots * HEADS * LENGTH // 2,
        ),
        name="attend",
    )(key_blocks, queries, chosen, *stored)


def blend_kernel(first, offsets, token_count, weight_count, *refs):
    blocks_ref, weight_place_ref = refs[:2]
    gain_ref, cosine_ref, sine_ref, chosen_ref, old_key_ref, old_value_ref = refs[2:8]
    cache_key_ref, cache_value_ref, cache_place_ref = refs[8:11]
    refs = refs[11:]
    token_refs, refs = refs[:token_count], refs[token_count:]
    weight_refs, refs = refs[:weight_count], refs[weight_count:]
    out_ref, fresh_key_ref, fresh_value_ref, held, weights, total, squares, queries = refs[-18:-10]
    keys, values, places, peak, denominator, numerator, score_slots = refs[-10:-3]
    token_sem, weight_sem, cache_sem = refs[-3:]
    step = pl.program_id(0)
    done = first * SLOTS
    blocks, slots, width = held.shape

    @pl.when(step == 0)
    def _():
        token_copies = []
        for piece, ref in enumerate(token_refs):
            for part in range(ref.shape[0]):
                number = len(token_copies)
                where = held.at[part, pl.ds(offsets[piece], ref.shape[1]), :]
                token_copies.append(pltpu.make_async_copy(ref.at[part], where, token_sem.at[number]))
        weight_copies = []
        for piece, ref in enumerate(weight_refs):
            start = pl.multiple_of(weight_place_ref[piece] * width, width)
            where = weights.at[pl.ds(start, ref.shape[0]), :]
            weight_copies.append(pltpu.make_async_copy(ref, where, weight_sem.at[piece]))
        fresh = fresh_key_ref.shape[0]
        cache_copies = [
            pltpu.make_async_copy(cache_key_ref, keys.at[pl.ds(0, LENGTH), :], cache_sem.at[0]),
            pltpu.make_async_copy(cache_value_ref, values.at[:, pl.ds(0, LENGTH)], cache_sem.at[1]),
            pltpu.make_async_copy(
                cache_place_ref.at[pl.ds(0, LENGTH + fresh), :], places, cache_sem.at[2]
            ),
        ]
        for copy in token_copies + weight_copies + cache_copies:
            copy.start()
        squares[...] = jnp.zeros_like(squares)
        number = 0
        for piece, ref in enumerate(token_refs):
            for block in range(ref.shape[0]):
                token_copies[number].wait()
                number += 1

                def add_squares(tile, carry, block=block, offset=offsets[piece]):
                    rows = pl.ds(pl.multiple_of(offset + tile * TILE, TILE), TILE)
                    hidden = held[block, rows, :].astype(jnp.float32)
                    hidden = hidden * hidden
                    part = hidden[:, :HD]
                    for start in range(HD, width, HD):
                        part = part + hidden[:, start : start + HD]
                    squares[rows, :] += part
                    return carry

                lax.fori_loop(0, ref.shape[1] // TILE, add_squares, 0)
        mean_square = jnp.sum(squares[...], axis=1, keepdims=True) * (1.0 / (blocks * width))
        squares[...] = jnp.broadcast_to(lax.rsqrt(mean_square + epsilon), squares.shape)
        for copy in weight_copies:
            copy.wait()
        height = slots // max(1, slots // ROWS)

        def project_rows(tile, carry):
            rows = pl.ds(pl.multiple_of(tile * height, height), height)
            scale = jnp.concatenate([squares[rows, :]] * (width // HD), axis=1)

            def add_blocks(group, carry):
                normed = []
                for part in range(GROUP):
                    block = group * GROUP + part
                    hidden = held[block, rows, :].astype(jnp.float32) * scale
                    normed.append(
                        (hidden * gain_ref[block].astype(jnp.float32)).astype(jnp.bfloat16)
                    )
                depth = GROUP * width
                start = pl.multiple_of(group * depth, depth)
                product = jnp.dot(
                    jnp.concatenate(normed, axis=1),
                    weights[pl.ds(start, depth), :],
                    preferred_element_type=jnp.float32,
                )
                total[rows, :] = jnp.where(group == 0, 0.0, total[rows, :]) + product
                return carry

            return lax.fori_loop(0, blocks // GROUP, add_blocks, carry)

        total[...] = jnp.zeros_like(total)
        lax.fori_loop(0, slots // height, project_rows, 0)
        cosine, signed_sine = cosine_ref[...], sine_ref[...]
        for head in range(HEADS):
            part = total[:, head * HD : (head + 1) * HD]
            queries[head] = rotate(part, cosine, signed_sine).astype(jnp.bfloat16)
        if done:
            fresh_key_ref[:done, :] = old_key_ref[:done, :]
            fresh_value_ref[:, :done] = old_value_ref[:, :done]
        fresh_key_ref[done : done + slots, :] = rotate(
            total[:, HEADS * HD : (HEADS + 1) * HD], cosine, signed_sine
        ).astype(jnp.bfloat16)
        fresh_value_ref[:, done : done + slots] = total[:, (HEADS + 1) * HD :].T.astype(jnp.bfloat16)
        if done + slots < fresh:
            fresh_key_ref[done + slots :, :] = jnp.zeros((fresh - done - slots, HD), jnp.bfloat16)
            fresh_value_ref[:, done + slots :] = jnp.zeros((HD, fresh - done - slots), jnp.bfloat16)
        keys[LENGTH:, :] = fresh_key_ref[...]
        values[:, LENGTH:] = fresh_value_ref[...]
        for copy in cache_copies:
            copy.wait()

    @pl.when(step > 0)
    def _():
        rows = HEADS * SLOTS
        own = pl.ds(pl.multiple_of((step - 1) * SLOTS, SLOTS), SLOTS)
        asked = queries[:, own, :].reshape(rows, HD)
        attend_slots(
            asked, chosen_ref[...], blocks_ref[step - 1], (first + step) * SLOTS,
            keys, values, places, out_ref, peak, denominator, numerator, score_slots,
        )


def blend(
    first, key_blocks, pieces, offsets, weight_pieces, weight_places, gain, cosine,
    signed_sine, chosen, old, keys, values, key_places, total_slots, earlier,
):
    slots = cosine.shape[0]
    width = pieces[0].shape[-1]
    blocks = gain.shape[0]
    columns = (HEADS + 2) * HD
    rows = HEADS * SLOTS
    fresh = -(-(first * SLOTS + slots) // KEYS) * KEYS

    def still(array):
        origin = (0,) * array.ndim
        return pl.BlockSpec(
            array.shape, lambda step, *tables: origin, pipeline_mode=pl.Buffered(1)
        )

    remote = pl.BlockSpec(memory_space=pl.ANY)
    operands = [
        key_blocks, weight_places, gain, cosine, signed_sine, chosen, *old,
        keys, values, key_places, *pieces, *weight_pieces, *earlier,
    ]
    return pl.pallas_call(
        functools.partial(blend_kernel, first, offsets, len(pieces), len(weight_pieces)),
        out_shape=(
            jax.ShapeDtypeStruct((total_slots, HEADS * HD), jnp.bfloat16),
            jax.ShapeDtypeStruct((fresh, HD), jnp.bfloat16),
            jax.ShapeDtypeStruct((HD, fresh), jnp.bfloat16),
        ),
        grid_spec=pltpu.PrefetchScalarGridSpec(
            num_scalar_prefetch=2,
            grid=(1 + slots // SLOTS,),
            in_specs=[
                still(gain),
                still(cosine),
                still(signed_sine),
                pl.BlockSpec((1, SLOTS), lambda step, *tables: (0, jnp.maximum(step - 1, 0))),
                still(old[0]),
                still(old[1]),
            ]
            + [remote] * (3 + len(pieces) + len(weight_pieces) + len(earlier)),
            out_specs=(
                pl.BlockSpec(
                    (SLOTS, HEADS * HD), lambda step, *tables: (first + jnp.maximum(step - 1, 0), 0)
                ),
                pl.BlockSpec((fresh, HD), lambda step, *tables: (0, 0)),
                pl.BlockSpec((HD, fresh), lambda step, *tables: (0, 0)),
            ),
            scratch_shapes=[
                pltpu.VMEM((blocks, slots, width), jnp.bfloat16),
                pltpu.VMEM((blocks * width, columns), jnp.bfloat16),
                pltpu.VMEM((slots, columns), jnp.float32),
                pltpu.VMEM((slots, HD), jnp.float32),
                pltpu.VMEM((HEADS, slots, HD), jnp.bfloat16),
                pltpu.VMEM((LENGTH + fresh, HD), jnp.bfloat16),
                pltpu.VMEM((HD, LENGTH + fresh), jnp.bfloat16),
                pltpu.VMEM((LENGTH + fresh, HD), jnp.int32),
                pltpu.VMEM((1, rows), jnp.float32),
                pltpu.VMEM((1, rows), jnp.float32),
                pltpu.VMEM((HD, rows), jnp.float32),
                pltpu.VMEM((2, KEYS, rows), jnp.float32),
                pltpu.SemaphoreType.DMA((blocks * len(pieces),)),
                pltpu.SemaphoreType.DMA((len(weight_pieces),)),
                pltpu.SemaphoreType.DMA((3,)),
            ],
        ),
        input_output_aliases={len(operands) - 1: 0} if earlier else {},
        compiler_params=pltpu.CompilerParams(vmem_limit_bytes=56 * 2**20),
        cost_estimate=pl.CostEstimate(
            flops=4 * slots * blocks * width * columns + slots * HEADS * LENGTH * HD * 2,
            bytes_accessed=2 * blocks * width * (slots + columns) + 8 * 2**20,
            transcendentals=slots * HEADS * LENGTH // 2,
        ),
        name="blend",
    )(*operands)


def ring(block, axis, shift):
    half = block.shape[-2] // 2
    behind = lax.ppermute(block, axis, shift(1))
    ahead = lax.ppermute(block, axis, shift(-1))
    far_first = lax.ppermute(behind[..., :half, :], axis, shift(1))
    far_second = lax.ppermute(ahead[..., half:, :], axis, shift(-1))
    return [block, behind, ahead, far_first, far_second]


def shards(tokens, norm_gain, w_query, w_keyval, kv_cache, selected, anchor):
    row_index = lax.axis_index("row")
    col_index = lax.axis_index("col")
    own_x, own_core = row_index // 2, row_index % 2
    holds_key = col_index % 2 == 0
    own_cache = kv_cache[0]
    chosen = selected[0]
    slot_count = chosen.shape[0]
    early = EARLY * SLOTS
    middle = NEAR * SPAN
    near_cache = lax.ppermute(own_cache[:middle], "col", flipped(16))
    early_tokens = lax.all_gather(tokens[0, :early], "col", axis=0)
    other_keyval = lax.ppermute(w_keyval, "col", flipped(16))
    late_tokens, other_keyval = lax.optimization_barrier((tokens[0, early:], other_keyval))
    late_tokens = lax.all_gather(late_tokens, "col", axis=0)
    far_cache, early_tokens = lax.optimization_barrier((own_cache[middle:], early_tokens))
    far_cache = lax.ppermute(far_cache, "col", flipped(16))

    weights = jnp.concatenate(
        [
            w_query,
            jnp.where(holds_key, w_keyval, other_keyval),
            jnp.where(holds_key, other_keyval, w_keyval),
        ],
        axis=1,
    )
    mine = ring(weights, "row", row_shift)
    theirs = [lax.ppermute(piece, "row", flipped(8)) for piece in mine]
    steps_x = jnp.array([0, 3, 1, 2, 2], jnp.int32)
    second_half = jnp.array([0, 0, 0, 0, 1], jnp.int32)
    source_x = (own_x + steps_x) % 4
    weight_places = jnp.concatenate(
        [
            (source_x * 2 + own_core) * 2 + second_half,
            (source_x * 2 + 1 - own_core) * 2 + second_half,
        ]
    )

    cosine, signed_sine = angles(chosen.astype(jnp.float32), HD)
    span_starts = jnp.arange(NCHUNK, dtype=jnp.int32) * SPAN - anchor[0]
    span_cosine, span_sine = angles(span_starts.astype(jnp.float32), HD)
    prepared = ()
    for first_span, partner in ((0, near_cache), (NEAR, far_cache)):
        prepared = prepare(
            first_span,
            holds_key.astype(jnp.int32)[None],
            own_cache,
            partner,
            span_cosine[:, None],
            span_sine[:, None],
            prepared,
        )
    keys, values = prepared
    padded = -(-slot_count // KEYS) * KEYS - slot_count
    key_places = mark(jnp.pad(chosen[None], ((0, 0), (0, padded)), constant_values=HIDDEN_POSITION))
    grouped = chosen.reshape(-1, SLOTS)
    farthest = jnp.max(jnp.where(grouped < LENGTH, grouped, -1), axis=1)
    key_blocks = (farthest + KEYS) // KEYS
    gain = norm_gain.reshape(NCHUNK, 1, -1)
    queries, *fresh = project(
        [early_tokens],
        (0,),
        gain,
        cosine[:early],
        signed_sine[:early],
        mine + theirs,
        weight_places,
        0,
    )
    attended = attend(
        0,
        key_blocks[:EARLY],
        queries,
        chosen[None, :early],
        (keys, values, key_places, *fresh),
        slot_count,
    )
    attended, late_tokens = lax.optimization_barrier((attended, late_tokens))
    attended, *_ = blend(
        EARLY,
        key_blocks[EARLY:],
        [late_tokens],
        (0,),
        mine + theirs,
        weight_places,
        gain,
        cosine[early:],
        signed_sine[early:],
        chosen[None, early:],
        fresh,
        keys,
        values,
        key_places,
        slot_count,
        (attended,),
    )
    return attended[None]


def solution(mesh):
    in_specs = (
        P("row", None, "col"),
        P(),
        P("row", "col"),
        P("row", "col"),
        P("row", None, "col"),
        P("row", None),
        P("row", None),
    )
    out_specs = P("row", None, "col")
    return jax.shard_map(shards, mesh=mesh, in_specs=in_specs, out_specs=out_specs, check_vma=False)
```

```python
import functools
import math

import jax
import jax.numpy as jnp
from jax import lax
from jax.experimental import pallas as pl
from jax.experimental.pallas import tpu as pltpu
from jax.sharding import PartitionSpec as P

HD = 128
SPAN = 512
NCHUNK = 16
LENGTH = SPAN * NCHUNK
HEADS = 4
KEYS = 512
SLOTS = 128
HIDDEN_POSITION = 4 * LENGTH
EARLY = 6
NEAR = 10
TILE = 64
ROWS = 384
GROUP = 4

rope_base = 500000.0
epsilon = 1e-05
masked_score = -1e30
exponent_scale = HD ** (-0.5) * math.log2(math.e)


def col_shift(dy, dz):
    return [(4 * y + z, 4 * ((y + dy) % 4) + (z + dz) % 4) for y in range(4) for z in range(4)]


def row_shift(dx):
    return [(2 * x + core, 2 * ((x + dx) % 4) + core) for x in range(4) for core in range(2)]


def flipped(count):
    return [(place, place ^ 1) for place in range(count)]


def angles(positions, width):
    half_width = width // 2
    exponents = jnp.arange(half_width, dtype=jnp.float32) * (-2.0 / width)
    frequency = jnp.exp(exponents * math.log(rope_base))
    phases = positions[..., None] * frequency
    cosine, sine_part = jnp.cos(phases), jnp.sin(phases)
    return (
        jnp.concatenate([cosine, cosine], axis=-1),
        jnp.concatenate([-sine_part, sine_part], axis=-1),
    )


def rotate(vectors, cosine, signed_sine):
    return vectors * cosine + pltpu.roll(vectors, HD // 2, 1) * signed_sine


def prepare_kernel(holds_key_ref, own_ref, partner_ref, cosine_ref, sine_ref, *refs):
    key_ref, value_ref = refs[-2:]
    holds_key = holds_key_ref[0] == 1
    own = own_ref[...]
    partner = partner_ref[...]
    stored_key = jnp.where(holds_key, own, partner).astype(jnp.float32)
    stored_value = jnp.where(holds_key, partner, own).astype(jnp.float32)
    key_ref[...] = rotate(stored_key, cosine_ref[0], sine_ref[0]).astype(jnp.bfloat16)
    value_ref[...] = stored_value.T.astype(jnp.bfloat16)


def mark_kernel(chosen_ref, place_ref):
    step = pl.program_id(0)

    @pl.when(step < NCHUNK)
    def _():
        place = step * SPAN + lax.broadcasted_iota(jnp.int32, (SPAN, HD), 0)
        seen = jnp.zeros((SPAN, HD), jnp.int32)
        for start in range(0, chosen_ref.shape[1], HD):
            seen = jnp.where(place == chosen_ref[0:1, start : start + HD], 1, seen)
        replaced = jnp.max(seen, axis=1, keepdims=True) > 0
        place_ref[...] = jnp.where(replaced, HIDDEN_POSITION, place)

    @pl.when(step >= NCHUNK)
    def _():
        for part in range(0, SPAN, HD):
            start = pl.multiple_of((step - NCHUNK) * SPAN + part, HD)
            fresh = jnp.broadcast_to(chosen_ref[0:1, pl.ds(start, HD)], (HD, HD))
            place_ref[part : part + HD, :] = fresh.astype(jnp.float32).T.astype(jnp.int32)


def mark(chosen):
    total = LENGTH + chosen.shape[1]
    return pl.pallas_call(
        mark_kernel,
        out_shape=jax.ShapeDtypeStruct((total, HD), jnp.int32),
        grid=(total // SPAN,),
        in_specs=[pl.BlockSpec((1, chosen.shape[1]), lambda step: (0, 0))],
        out_specs=pl.BlockSpec((SPAN, HD), lambda step: (step, 0)),
        cost_estimate=pl.CostEstimate(flops=10**7, bytes_accessed=5 * 2**20, transcendentals=0),
        name="mark",
    )(chosen)


def prepare(first, holds_key, own, partner, cosine, signed_sine, earlier):
    block = pl.BlockSpec((SPAN, HD), lambda step, flag: (first + step, 0))
    angle = pl.BlockSpec((1, 1, HD), lambda step, flag: (first + step, 0, 0))
    return pl.pallas_call(
        prepare_kernel,
        out_shape=(
            jax.ShapeDtypeStruct((LENGTH, HD), jnp.bfloat16),
            jax.ShapeDtypeStruct((HD, LENGTH), jnp.bfloat16),
        ),
        grid_spec=pltpu.PrefetchScalarGridSpec(
            num_scalar_prefetch=1,
            grid=(partner.shape[0] // SPAN,),
            in_specs=[
                block,
                pl.BlockSpec((SPAN, HD), lambda step, flag: (step, 0)),
                angle,
                angle,
            ]
            + [pl.BlockSpec(memory_space=pl.ANY)] * len(earlier),
            out_specs=(
                block,
                pl.BlockSpec((HD, SPAN), lambda step, flag: (0, first + step)),
            ),
        ),
        input_output_aliases={5 + number: number for number in range(len(earlier))},
        cost_estimate=pl.CostEstimate(flops=10**7, bytes_accessed=6 * 2**20, transcendentals=0),
        name="prepare",
    )(holds_key, own, partner, cosine, signed_sine, *earlier)


def project_kernel(offsets, token_count, weight_count, done, *refs):
    weight_place_ref, gain_ref, cosine_ref, sine_ref = refs[:4]
    refs = refs[4:]
    token_refs, refs = refs[:token_count], refs[token_count:]
    weight_refs, refs = refs[:weight_count], refs[weight_count:]
    query_ref, key_ref, value_ref, held, weights, total, squares, token_sem, weight_sem = refs
    blocks, slots, width = held.shape
    token_copies = []
    for piece, ref in enumerate(token_refs):
        for part in range(ref.shape[0]):
            number = len(token_copies)
            where = held.at[part, pl.ds(offsets[piece], ref.shape[1]), :]
            token_copies.append(pltpu.make_async_copy(ref.at[part], where, token_sem.at[number]))
    weight_copies = []
    for piece, ref in enumerate(weight_refs):
        start = pl.multiple_of(weight_place_ref[piece] * width, width)
        where = weights.at[pl.ds(start, ref.shape[0]), :]
        weight_copies.append(pltpu.make_async_copy(ref, where, weight_sem.at[piece]))
    for copy in token_copies:
        copy.start()
    squares[...] = jnp.zeros_like(squares)
    number = 0
    for piece, ref in enumerate(token_refs):
        for block in range(ref.shape[0]):
            if number == len(token_copies) // 2:
                for copy in weight_copies:
                    copy.start()
            token_copies[number].wait()
            number += 1

            def add_squares(tile, carry, block=block, offset=offsets[piece]):
                rows = pl.ds(pl.multiple_of(offset + tile * TILE, TILE), TILE)
                hidden = held[block, rows, :].astype(jnp.float32)
                hidden = hidden * hidden
                part = hidden[:, :HD]
                for start in range(HD, width, HD):
                    part = part + hidden[:, start : start + HD]
                squares[rows, :] += part
                return carry

            lax.fori_loop(0, ref.shape[1] // TILE, add_squares, 0)
    mean_square = jnp.sum(squares[...], axis=1, keepdims=True) * (1.0 / (blocks * width))
    squares[...] = jnp.broadcast_to(lax.rsqrt(mean_square + epsilon), squares.shape)
    for copy in weight_copies:
        copy.wait()

    height = slots // max(1, slots // ROWS)

    def project_rows(tile, carry):
        rows = pl.ds(pl.multiple_of(tile * height, height), height)
        scale = jnp.concatenate([squares[rows, :]] * (width // HD), axis=1)

        def add_blocks(group, carry):
            normed = []
            for part in range(GROUP):
                block = group * GROUP + part
                hidden = held[block, rows, :].astype(jnp.float32) * scale
                normed.append((hidden * gain_ref[block].astype(jnp.float32)).astype(jnp.bfloat16))
            depth = GROUP * width
            start = pl.multiple_of(group * depth, depth)
            product = jnp.dot(
                jnp.concatenate(normed, axis=1),
                weights[pl.ds(start, depth), :],
                preferred_element_type=jnp.float32,
            )
            total[rows, :] = jnp.where(group == 0, 0.0, total[rows, :]) + product
            return carry

        return lax.fori_loop(0, blocks // GROUP, add_blocks, carry)

    total[...] = jnp.zeros_like(total)
    lax.fori_loop(0, slots // height, project_rows, 0)
    cosine, signed_sine = cosine_ref[...], sine_ref[...]
    for head in range(HEADS):
        part = total[:, head * HD : (head + 1) * HD]
        query_ref[head] = rotate(part, cosine, signed_sine).astype(jnp.bfloat16)
    key_ref[done : done + slots, :] = rotate(
        total[:, HEADS * HD : (HEADS + 1) * HD], cosine, signed_sine
    ).astype(jnp.bfloat16)
    value_ref[:, done : done + slots] = total[:, (HEADS + 1) * HD :].T.astype(jnp.bfloat16)
    if done + slots < key_ref.shape[0]:
        key_ref[done + slots :, :] = jnp.zeros_like(key_ref[done + slots :, :])
        value_ref[:, done + slots :] = jnp.zeros_like(value_ref[:, done + slots :])


def project(token_pieces, offsets, gain, cosine, signed_sine, weight_pieces, weight_places, done):
    slots = cosine.shape[0]
    width = token_pieces[0].shape[-1]
    blocks = gain.shape[0]
    columns = (HEADS + 2) * HD
    fresh = -(-(done + slots) // KEYS) * KEYS
    whole = pl.BlockSpec(memory_space=pltpu.VMEM)
    remote = pl.BlockSpec(memory_space=pl.ANY)
    scalars = pl.BlockSpec(memory_space=pltpu.SMEM)
    return pl.pallas_call(
        functools.partial(project_kernel, offsets, len(token_pieces), len(weight_pieces), done),
        out_shape=(
            jax.ShapeDtypeStruct((HEADS, slots, HD), jnp.bfloat16),
            jax.ShapeDtypeStruct((fresh, HD), jnp.bfloat16),
            jax.ShapeDtypeStruct((HD, fresh), jnp.bfloat16),
        ),
        in_specs=[scalars, whole, whole, whole]
        + [remote] * (len(token_pieces) + len(weight_pieces)),
        out_specs=(whole, whole, whole),
        scratch_shapes=[
            pltpu.VMEM((blocks, slots, width), jnp.bfloat16),
            pltpu.VMEM((blocks * width, columns), jnp.bfloat16),
            pltpu.VMEM((slots, columns), jnp.float32),
            pltpu.VMEM((slots, HD), jnp.float32),
            pltpu.SemaphoreType.DMA((blocks * len(token_pieces),)),
            pltpu.SemaphoreType.DMA((len(weight_pieces),)),
        ],
        compiler_params=pltpu.CompilerParams(vmem_limit_bytes=48 * 2**20),
        cost_estimate=pl.CostEstimate(
            flops=4 * slots * blocks * width * columns,
            bytes_accessed=2 * blocks * width * (slots + columns),
            transcendentals=0,
        ),
        name="project",
    )(weight_places, gain, cosine, signed_sine, *token_pieces, *weight_pieces)


def attend_slots(
    asked, chosen, stored, slots_seen, keys, values, places, out_ref, peak, denominator, numerator, score_slots
):
    limit = jnp.concatenate([chosen] * HEADS, axis=1)
    peak[...] = jnp.full_like(peak, masked_score)
    denominator[...] = jnp.zeros_like(denominator)
    numerator[...] = jnp.zeros_like(numerator)
    count = stored + (slots_seen + KEYS - 1) // KEYS

    def start_of(block):
        block = jnp.minimum(block, count - 1)
        block = jnp.where(block < stored, block, block - stored + LENGTH // KEYS)
        return pl.multiple_of(block * KEYS, KEYS)

    def score(block, slot):
        score_slots[slot] = lax.dot_general(
            keys[pl.ds(start_of(block), KEYS), :],
            asked,
            (((1,), (1,)), ((), ())),
            preferred_element_type=jnp.float32,
        )

    def gather(block, slot):
        start = start_of(block)
        place = jnp.concatenate([places[pl.ds(start, KEYS), :]] * HEADS, axis=1)
        scores = jnp.where(place <= limit, score_slots[slot], masked_score)
        old_peak = peak[...]
        new_peak = jnp.maximum(old_peak, jnp.max(scores, axis=0, keepdims=True))
        rescale = jnp.exp2((old_peak - new_peak) * exponent_scale)
        exponentials = jnp.exp2((scores - new_peak) * exponent_scale)
        denominator[...] = denominator[...] * rescale + jnp.sum(
            exponentials, axis=0, keepdims=True
        )
        numerator[...] = numerator[...] * rescale + jnp.dot(
            values[:, pl.ds(start, KEYS)],
            exponentials.astype(jnp.bfloat16),
            preferred_element_type=jnp.float32,
        )
        peak[...] = new_peak

    score(0, 0)

    def pair(turn, carry):
        block = 2 * turn
        score(block + 1, 1)
        gather(block, 0)
        score(block + 2, 0)
        gather(block + 1, 1)
        return carry

    lax.fori_loop(0, count // 2, pair, 0)

    @pl.when(count % 2 == 1)
    def _():
        gather(count - 1, 0)

    outcome = jnp.where(limit < LENGTH, numerator[...] / denominator[...], 0.0)
    for head in range(HEADS):
        part = outcome[:, head * SLOTS : (head + 1) * SLOTS]
        out_ref[:, head * HD : (head + 1) * HD] = part.T.astype(jnp.bfloat16)


def attend_kernel(first, blocks_ref, query_ref, chosen_ref, *refs):
    stored_refs, (out_ref, *scratch) = refs[:5], refs[-9:]
    keys, values, places, peak, denominator, numerator, score_slots, sem = scratch
    step = pl.program_id(0)
    fresh = stored_refs[3].shape[0]

    @pl.when(step == 0)
    def _():
        old, new = pl.ds(0, LENGTH), pl.ds(LENGTH, fresh)
        wheres = (keys.at[old, :], values.at[:, old], places, keys.at[new, :], values.at[:, new])
        held_places = stored_refs[2].at[pl.ds(0, LENGTH + fresh), :]
        sources = (*stored_refs[:2], held_places, *stored_refs[3:])
        copies = [
            pltpu.make_async_copy(source, where, sem.at[number])
            for number, (source, where) in enumerate(zip(sources, wheres))
        ]
        for copy in copies:
            copy.start()
        for copy in copies:
            copy.wait()

    attend_slots(
        query_ref[...].reshape(HEADS * SLOTS, HD), chosen_ref[...], blocks_ref[step],
        (first + step + 1) * SLOTS,
        keys, values, places, out_ref, peak, denominator, numerator, score_slots,
    )


def attend(first, key_blocks, queries, chosen, stored, total_slots):
    slots = queries.shape[1]
    rows = HEADS * SLOTS
    length = LENGTH + stored[3].shape[0]
    return pl.pallas_call(
        functools.partial(attend_kernel, first),
        out_shape=jax.ShapeDtypeStruct((total_slots, HEADS * HD), jnp.bfloat16),
        grid_spec=pltpu.PrefetchScalarGridSpec(
            num_scalar_prefetch=1,
            grid=(slots // SLOTS,),
            in_specs=[
                pl.BlockSpec((HEADS, SLOTS, HD), lambda step, counts: (0, step, 0)),
                pl.BlockSpec((1, SLOTS), lambda step, counts: (0, step)),
            ]
            + [pl.BlockSpec(memory_space=pl.ANY)] * 5,
            out_specs=pl.BlockSpec((SLOTS, HEADS * HD), lambda step, counts: (first + step, 0)),
            scratch_shapes=[
                pltpu.VMEM((length, HD), jnp.bfloat16),
                pltpu.VMEM((HD, length), jnp.bfloat16),
                pltpu.VMEM((length, HD), jnp.int32),
                pltpu.VMEM((1, rows), jnp.float32),
                pltpu.VMEM((1, rows), jnp.float32),
                pltpu.VMEM((HD, rows), jnp.float32),
                pltpu.VMEM((2, KEYS, rows), jnp.float32),
                pltpu.SemaphoreType.DMA((5,)),
            ],
        ),
        compiler_params=pltpu.CompilerParams(vmem_limit_bytes=56 * 2**20),
        cost_estimate=pl.CostEstimate(
            flops=slots * HEADS * LENGTH * HD * 2,
            bytes_accessed=12 * 2**20,
            transcendentals=slots * HEADS * LENGTH // 2,
        ),
        name="attend",
    )(key_blocks, queries, chosen, *stored)


def blend_kernel(first, offsets, token_count, weight_count, *refs):
    blocks_ref, weight_place_ref = refs[:2]
    gain_ref, cosine_ref, sine_ref, chosen_ref, old_key_ref, old_value_ref = refs[2:8]
    cache_key_ref, cache_value_ref, cache_place_ref = refs[8:11]
    refs = refs[11:]
    token_refs, refs = refs[:token_count], refs[token_count:]
    weight_refs, refs = refs[:weight_count], refs[weight_count:]
    out_ref, fresh_key_ref, fresh_value_ref, held, weights, total, squares, queries = refs[-18:-10]
    keys, values, places, peak, denominator, numerator, score_slots = refs[-10:-3]
    token_sem, weight_sem, cache_sem = refs[-3:]
    step = pl.program_id(0)
    done = first * SLOTS
    blocks, slots, width = held.shape

    @pl.when(step == 0)
    def _():
        token_copies = []
        for piece, ref in enumerate(token_refs):
            for part in range(ref.shape[0]):
                number = len(token_copies)
                where = held.at[part, pl.ds(offsets[piece], ref.shape[1]), :]
                token_copies.append(pltpu.make_async_copy(ref.at[part], where, token_sem.at[number]))
        weight_copies = []
        for piece, ref in enumerate(weight_refs):
            start = pl.multiple_of(weight_place_ref[piece] * width, width)
            where = weights.at[pl.ds(start, ref.shape[0]), :]
            weight_copies.append(pltpu.make_async_copy(ref, where, weight_sem.at[piece]))
        fresh = fresh_key_ref.shape[0]
        cache_copies = [
            pltpu.make_async_copy(cache_key_ref, keys.at[pl.ds(0, LENGTH), :], cache_sem.at[0]),
            pltpu.make_async_copy(cache_value_ref, values.at[:, pl.ds(0, LENGTH)], cache_sem.at[1]),
            pltpu.make_async_copy(
                cache_place_ref.at[pl.ds(0, LENGTH + fresh), :], places, cache_sem.at[2]
            ),
        ]
        for copy in token_copies:
            copy.start()
        squares[...] = jnp.zeros_like(squares)
        number = 0
        for piece, ref in enumerate(token_refs):
            for block in range(ref.shape[0]):
                if number == len(token_copies) // 2:
                    for copy in weight_copies:
                        copy.start()
                token_copies[number].wait()
                number += 1

                def add_squares(tile, carry, block=block, offset=offsets[piece]):
                    rows = pl.ds(pl.multiple_of(offset + tile * TILE, TILE), TILE)
                    hidden = held[block, rows, :].astype(jnp.float32)
                    hidden = hidden * hidden
                    part = hidden[:, :HD]
                    for start in range(HD, width, HD):
                        part = part + hidden[:, start : start + HD]
                    squares[rows, :] += part
                    return carry

                lax.fori_loop(0, ref.shape[1] // TILE, add_squares, 0)
        mean_square = jnp.sum(squares[...], axis=1, keepdims=True) * (1.0 / (blocks * width))
        squares[...] = jnp.broadcast_to(lax.rsqrt(mean_square + epsilon), squares.shape)
        for copy in weight_copies:
            copy.wait()
        for copy in cache_copies:
            copy.start()
        height = slots // max(1, slots // ROWS)

        def project_rows(tile, carry):
            rows = pl.ds(pl.multiple_of(tile * height, height), height)
            scale = jnp.concatenate([squares[rows, :]] * (width // HD), axis=1)

            def add_blocks(group, carry):
                normed = []
                for part in range(GROUP):
                    block = group * GROUP + part
                    hidden = held[block, rows, :].astype(jnp.float32) * scale
                    normed.append(
                        (hidden * gain_ref[block].astype(jnp.float32)).astype(jnp.bfloat16)
                    )
                depth = GROUP * width
                start = pl.multiple_of(group * depth, depth)
                product = jnp.dot(
                    jnp.concatenate(normed, axis=1),
                    weights[pl.ds(start, depth), :],
                    preferred_element_type=jnp.float32,
                )
                total[rows, :] = jnp.where(group == 0, 0.0, total[rows, :]) + product
                return carry

            return lax.fori_loop(0, blocks // GROUP, add_blocks, carry)

        total[...] = jnp.zeros_like(total)
        lax.fori_loop(0, slots // height, project_rows, 0)
        cosine, signed_sine = cosine_ref[...], sine_ref[...]
        for head in range(HEADS):
            part = total[:, head * HD : (head + 1) * HD]
            queries[head] = rotate(part, cosine, signed_sine).astype(jnp.bfloat16)
        if done:
            fresh_key_ref[:done, :] = old_key_ref[:done, :]
            fresh_value_ref[:, :done] = old_value_ref[:, :done]
        fresh_key_ref[done : done + slots, :] = rotate(
            total[:, HEADS * HD : (HEADS + 1) * HD], cosine, signed_sine
        ).astype(jnp.bfloat16)
        fresh_value_ref[:, done : done + slots] = total[:, (HEADS + 1) * HD :].T.astype(jnp.bfloat16)
        if done + slots < fresh:
            fresh_key_ref[done + slots :, :] = jnp.zeros((fresh - done - slots, HD), jnp.bfloat16)
            fresh_value_ref[:, done + slots :] = jnp.zeros((HD, fresh - done - slots), jnp.bfloat16)
        keys[LENGTH:, :] = fresh_key_ref[...]
        values[:, LENGTH:] = fresh_value_ref[...]
        for copy in cache_copies:
            copy.wait()

    @pl.when(step > 0)
    def _():
        rows = HEADS * SLOTS
        own = pl.ds(pl.multiple_of((step - 1) * SLOTS, SLOTS), SLOTS)
        asked = queries[:, own, :].reshape(rows, HD)
        attend_slots(
            asked, chosen_ref[...], blocks_ref[step - 1], (first + step) * SLOTS,
            keys, values, places, out_ref, peak, denominator, numerator, score_slots,
        )


def blend(
    first, key_blocks, pieces, offsets, weight_pieces, weight_places, gain, cosine,
    signed_sine, chosen, old, keys, values, key_places, total_slots, earlier,
):
    slots = cosine.shape[0]
    width = pieces[0].shape[-1]
    blocks = gain.shape[0]
    columns = (HEADS + 2) * HD
    rows = HEADS * SLOTS
    fresh = -(-(first * SLOTS + slots) // KEYS) * KEYS

    def still(array):
        origin = (0,) * array.ndim
        return pl.BlockSpec(
            array.shape, lambda step, *tables: origin, pipeline_mode=pl.Buffered(1)
        )

    remote = pl.BlockSpec(memory_space=pl.ANY)
    operands = [
        key_blocks, weight_places, gain, cosine, signed_sine, chosen, *old,
        keys, values, key_places, *pieces, *weight_pieces, *earlier,
    ]
    return pl.pallas_call(
        functools.partial(blend_kernel, first, offsets, len(pieces), len(weight_pieces)),
        out_shape=(
            jax.ShapeDtypeStruct((total_slots, HEADS * HD), jnp.bfloat16),
            jax.ShapeDtypeStruct((fresh, HD), jnp.bfloat16),
            jax.ShapeDtypeStruct((HD, fresh), jnp.bfloat16),
        ),
        grid_spec=pltpu.PrefetchScalarGridSpec(
            num_scalar_prefetch=2,
            grid=(1 + slots // SLOTS,),
            in_specs=[
                still(gain),
                still(cosine),
                still(signed_sine),
                pl.BlockSpec((1, SLOTS), lambda step, *tables: (0, jnp.maximum(step - 1, 0))),
                still(old[0]),
                still(old[1]),
            ]
            + [remote] * (3 + len(pieces) + len(weight_pieces) + len(earlier)),
            out_specs=(
                pl.BlockSpec(
                    (SLOTS, HEADS * HD), lambda step, *tables: (first + jnp.maximum(step - 1, 0), 0)
                ),
                pl.BlockSpec((fresh, HD), lambda step, *tables: (0, 0)),
                pl.BlockSpec((HD, fresh), lambda step, *tables: (0, 0)),
            ),
            scratch_shapes=[
                pltpu.VMEM((blocks, slots, width), jnp.bfloat16),
                pltpu.VMEM((blocks * width, columns), jnp.bfloat16),
                pltpu.VMEM((slots, columns), jnp.float32),
                pltpu.VMEM((slots, HD), jnp.float32),
                pltpu.VMEM((HEADS, slots, HD), jnp.bfloat16),
                pltpu.VMEM((LENGTH + fresh, HD), jnp.bfloat16),
                pltpu.VMEM((HD, LENGTH + fresh), jnp.bfloat16),
                pltpu.VMEM((LENGTH + fresh, HD), jnp.int32),
                pltpu.VMEM((1, rows), jnp.float32),
                pltpu.VMEM((1, rows), jnp.float32),
                pltpu.VMEM((HD, rows), jnp.float32),
                pltpu.VMEM((2, KEYS, rows), jnp.float32),
                pltpu.SemaphoreType.DMA((blocks * len(pieces),)),
                pltpu.SemaphoreType.DMA((len(weight_pieces),)),
                pltpu.SemaphoreType.DMA((3,)),
            ],
        ),
        input_output_aliases={len(operands) - 1: 0} if earlier else {},
        compiler_params=pltpu.CompilerParams(vmem_limit_bytes=56 * 2**20),
        cost_estimate=pl.CostEstimate(
            flops=4 * slots * blocks * width * columns + slots * HEADS * LENGTH * HD * 2,
            bytes_accessed=2 * blocks * width * (slots + columns) + 8 * 2**20,
            transcendentals=slots * HEADS * LENGTH // 2,
        ),
        name="blend",
    )(*operands)


def ring(block, axis, shift):
    half = block.shape[-2] // 2
    behind = lax.ppermute(block, axis, shift(1))
    ahead = lax.ppermute(block, axis, shift(-1))
    far_first = lax.ppermute(behind[..., :half, :], axis, shift(1))
    far_second = lax.ppermute(ahead[..., half:, :], axis, shift(-1))
    return [block, behind, ahead, far_first, far_second]


def shards(tokens, norm_gain, w_query, w_keyval, kv_cache, selected, anchor):
    row_index = lax.axis_index("row")
    col_index = lax.axis_index("col")
    own_x, own_core = row_index // 2, row_index % 2
    holds_key = col_index % 2 == 0
    own_cache = kv_cache[0]
    chosen = selected[0]
    slot_count = chosen.shape[0]
    early = EARLY * SLOTS
    middle = NEAR * SPAN
    near_cache = lax.ppermute(own_cache[:middle], "col", flipped(16))
    early_tokens = lax.all_gather(tokens[0, :early], "col", axis=0)
    other_keyval = lax.ppermute(w_keyval, "col", flipped(16))
    late_tokens, other_keyval = lax.optimization_barrier((tokens[0, early:], other_keyval))
    late_tokens = lax.all_gather(late_tokens, "col", axis=0)
    far_cache, early_tokens = lax.optimization_barrier((own_cache[middle:], early_tokens))
    far_cache = lax.ppermute(far_cache, "col", flipped(16))

    weights = jnp.concatenate(
        [
            w_query,
            jnp.where(holds_key, w_keyval, other_keyval),
            jnp.where(holds_key, other_keyval, w_keyval),
        ],
        axis=1,
    )
    mine = ring(weights, "row", row_shift)
    theirs = [lax.ppermute(piece, "row", flipped(8)) for piece in mine]
    steps_x = jnp.array([0, 3, 1, 2, 2], jnp.int32)
    second_half = jnp.array([0, 0, 0, 0, 1], jnp.int32)
    source_x = (own_x + steps_x) % 4
    weight_places = jnp.concatenate(
        [
            (source_x * 2 + own_core) * 2 + second_half,
            (source_x * 2 + 1 - own_core) * 2 + second_half,
        ]
    )

    cosine, signed_sine = angles(chosen.astype(jnp.float32), HD)
    span_starts = jnp.arange(NCHUNK, dtype=jnp.int32) * SPAN - anchor[0]
    span_cosine, span_sine = angles(span_starts.astype(jnp.float32), HD)
    prepared = ()
    for first_span, partner in ((0, near_cache), (NEAR, far_cache)):
        prepared = prepare(
            first_span,
            holds_key.astype(jnp.int32)[None],
            own_cache,
            partner,
            span_cosine[:, None],
            span_sine[:, None],
            prepared,
        )
    keys, values = prepared
    padded = -(-slot_count // KEYS) * KEYS - slot_count
    key_places = mark(jnp.pad(chosen[None], ((0, 0), (0, padded)), constant_values=HIDDEN_POSITION))
    grouped = chosen.reshape(-1, SLOTS)
    farthest = jnp.max(jnp.where(grouped < LENGTH, grouped, -1), axis=1)
    key_blocks = (farthest + KEYS) // KEYS
    gain = norm_gain.reshape(NCHUNK, 1, -1)
    queries, *fresh = project(
        [early_tokens],
        (0,),
        gain,
        cosine[:early],
        signed_sine[:early],
        mine + theirs,
        weight_places,
        0,
    )
    attended = attend(
        0,
        key_blocks[:EARLY],
        queries,
        chosen[None, :early],
        (keys, values, key_places, *fresh),
        slot_count,
    )
    attended, late_tokens = lax.optimization_barrier((attended, late_tokens))
    attended, *_ = blend(
        EARLY,
        key_blocks[EARLY:],
        [late_tokens],
        (0,),
        mine + theirs,
        weight_places,
        gain,
        cosine[early:],
        signed_sine[early:],
        chosen[None, early:],
        fresh,
        keys,
        values,
        key_places,
        slot_count,
        (attended,),
    )
    return attended[None]


def solution(mesh):
    in_specs = (
        P("row", None, "col"),
        P(),
        P("row", "col"),
        P("row", "col"),
        P("row", None, "col"),
        P("row", None),
        P("row", None),
    )
    out_specs = P("row", None, "col")
    return jax.shard_map(shards, mesh=mesh, in_specs=in_specs, out_specs=out_specs, check_vma=False)
```

```python
import functools
import math

import jax
import jax.numpy as jnp
from jax import lax
from jax.experimental import pallas as pl
from jax.experimental.pallas import tpu as pltpu
from jax.sharding import PartitionSpec as P

HD = 128
SPAN = 512
NCHUNK = 16
LENGTH = SPAN * NCHUNK
HEADS = 4
KEYS = 512
SLOTS = 128
HIDDEN_POSITION = 4 * LENGTH
EARLY = 6
NEAR = 10
TILE = 192
ROWS = 384
GROUP = 8

rope_base = 500000.0
epsilon = 1e-05
masked_score = -1e30
exponent_scale = HD ** (-0.5) * math.log2(math.e)


def col_shift(dy, dz):
    return [(4 * y + z, 4 * ((y + dy) % 4) + (z + dz) % 4) for y in range(4) for z in range(4)]


def row_shift(dx):
    return [(2 * x + core, 2 * ((x + dx) % 4) + core) for x in range(4) for core in range(2)]


def flipped(count):
    return [(place, place ^ 1) for place in range(count)]


def angles(positions, width):
    half_width = width // 2
    exponents = jnp.arange(half_width, dtype=jnp.float32) * (-2.0 / width)
    frequency = jnp.exp(exponents * math.log(rope_base))
    phases = positions[..., None] * frequency
    cosine, sine_part = jnp.cos(phases), jnp.sin(phases)
    return (
        jnp.concatenate([cosine, cosine], axis=-1),
        jnp.concatenate([-sine_part, sine_part], axis=-1),
    )


def rotate(vectors, cosine, signed_sine):
    return vectors * cosine + pltpu.roll(vectors, HD // 2, 1) * signed_sine


def prepare_kernel(holds_key_ref, own_ref, partner_ref, cosine_ref, sine_ref, *refs):
    key_ref, value_ref = refs[-2:]
    holds_key = holds_key_ref[0] == 1
    own = own_ref[...]
    partner = partner_ref[...]
    stored_key = jnp.where(holds_key, own, partner).astype(jnp.float32)
    stored_value = jnp.where(holds_key, partner, own).astype(jnp.float32)
    key_ref[...] = rotate(stored_key, cosine_ref[0], sine_ref[0]).astype(jnp.bfloat16)
    value_ref[...] = stored_value.T.astype(jnp.bfloat16)


def mark_kernel(chosen_ref, place_ref):
    step = pl.program_id(0)

    @pl.when(step < NCHUNK)
    def _():
        place = step * SPAN + lax.broadcasted_iota(jnp.int32, (SPAN, HD), 0)
        seen = jnp.zeros((SPAN, HD), jnp.int32)
        for start in range(0, chosen_ref.shape[1], HD):
            seen = jnp.where(place == chosen_ref[0:1, start : start + HD], 1, seen)
        replaced = jnp.max(seen, axis=1, keepdims=True) > 0
        place_ref[...] = jnp.where(replaced, HIDDEN_POSITION, place)

    @pl.when(step >= NCHUNK)
    def _():
        for part in range(0, SPAN, HD):
            start = pl.multiple_of((step - NCHUNK) * SPAN + part, HD)
            fresh = jnp.broadcast_to(chosen_ref[0:1, pl.ds(start, HD)], (HD, HD))
            place_ref[part : part + HD, :] = fresh.astype(jnp.float32).T.astype(jnp.int32)


def mark(chosen):
    total = LENGTH + chosen.shape[1]
    return pl.pallas_call(
        mark_kernel,
        out_shape=jax.ShapeDtypeStruct((total, HD), jnp.int32),
        grid=(total // SPAN,),
        in_specs=[pl.BlockSpec((1, chosen.shape[1]), lambda step: (0, 0))],
        out_specs=pl.BlockSpec((SPAN, HD), lambda step: (step, 0)),
        cost_estimate=pl.CostEstimate(flops=10**7, bytes_accessed=5 * 2**20, transcendentals=0),
        name="mark",
    )(chosen)


def prepare(first, holds_key, own, partner, cosine, signed_sine, earlier):
    block = pl.BlockSpec((SPAN, HD), lambda step, flag: (first + step, 0))
    angle = pl.BlockSpec((1, 1, HD), lambda step, flag: (first + step, 0, 0))
    return pl.pallas_call(
        prepare_kernel,
        out_shape=(
            jax.ShapeDtypeStruct((LENGTH, HD), jnp.bfloat16),
            jax.ShapeDtypeStruct((HD, LENGTH), jnp.bfloat16),
        ),
        grid_spec=pltpu.PrefetchScalarGridSpec(
            num_scalar_prefetch=1,
            grid=(partner.shape[0] // SPAN,),
            in_specs=[
                block,
                pl.BlockSpec((SPAN, HD), lambda step, flag: (step, 0)),
                angle,
                angle,
            ]
            + [pl.BlockSpec(memory_space=pl.ANY)] * len(earlier),
            out_specs=(
                block,
                pl.BlockSpec((HD, SPAN), lambda step, flag: (0, first + step)),
            ),
        ),
        input_output_aliases={5 + number: number for number in range(len(earlier))},
        cost_estimate=pl.CostEstimate(flops=10**7, bytes_accessed=6 * 2**20, transcendentals=0),
        name="prepare",
    )(holds_key, own, partner, cosine, signed_sine, *earlier)


def project_kernel(offsets, token_count, weight_count, done, *refs):
    weight_place_ref, gain_ref, cosine_ref, sine_ref = refs[:4]
    refs = refs[4:]
    token_refs, refs = refs[:token_count], refs[token_count:]
    weight_refs, refs = refs[:weight_count], refs[weight_count:]
    query_ref, key_ref, value_ref, held, weights, total, squares, token_sem, weight_sem = refs
    blocks, slots, width = held.shape
    token_copies = []
    for piece, ref in enumerate(token_refs):
        for part in range(ref.shape[0]):
            number = len(token_copies)
            where = held.at[part, pl.ds(offsets[piece], ref.shape[1]), :]
            token_copies.append(pltpu.make_async_copy(ref.at[part], where, token_sem.at[number]))
    weight_copies = []
    for piece, ref in enumerate(weight_refs):
        start = pl.multiple_of(weight_place_ref[piece] * width, width)
        where = weights.at[pl.ds(start, ref.shape[0]), :]
        weight_copies.append(pltpu.make_async_copy(ref, where, weight_sem.at[piece]))
    for copy in token_copies:
        copy.start()
    squares[...] = jnp.zeros_like(squares)
    number = 0
    for piece, ref in enumerate(token_refs):
        for block in range(ref.shape[0]):
            if number == len(token_copies) // 4:
                for copy in weight_copies:
                    copy.start()
            token_copies[number].wait()
            number += 1

            def add_squares(tile, carry, block=block, offset=offsets[piece]):
                rows = pl.ds(pl.multiple_of(offset + tile * TILE, TILE), TILE)
                hidden = held[block, rows, :].astype(jnp.float32)
                hidden = hidden * hidden
                part = hidden[:, :HD]
                for start in range(HD, width, HD):
                    part = part + hidden[:, start : start + HD]
                squares[rows, :] += part
                return carry

            lax.fori_loop(0, ref.shape[1] // TILE, add_squares, 0)
    mean_square = jnp.sum(squares[...], axis=1, keepdims=True) * (1.0 / (blocks * width))
    squares[...] = jnp.broadcast_to(lax.rsqrt(mean_square + epsilon), squares.shape)
    for copy in weight_copies:
        copy.wait()

    height = slots // max(1, slots // ROWS)

    def project_rows(tile, carry):
        rows = pl.ds(pl.multiple_of(tile * height, height), height)
        scale = jnp.concatenate([squares[rows, :]] * (width // HD), axis=1)

        def add_blocks(group, carry):
            normed = []
            for part in range(GROUP):
                block = group * GROUP + part
                hidden = held[block, rows, :].astype(jnp.float32) * scale
                normed.append((hidden * gain_ref[block].astype(jnp.float32)).astype(jnp.bfloat16))
            depth = GROUP * width
            start = pl.multiple_of(group * depth, depth)
            product = jnp.dot(
                jnp.concatenate(normed, axis=1),
                weights[pl.ds(start, depth), :],
                preferred_element_type=jnp.float32,
            )
            total[rows, :] = jnp.where(group == 0, 0.0, total[rows, :]) + product
            return carry

        return lax.fori_loop(0, blocks // GROUP, add_blocks, carry)

    total[...] = jnp.zeros_like(total)
    lax.fori_loop(0, slots // height, project_rows, 0)
    cosine, signed_sine = cosine_ref[...], sine_ref[...]
    for head in range(HEADS):
        part = total[:, head * HD : (head + 1) * HD]
        query_ref[head] = rotate(part, cosine, signed_sine).astype(jnp.bfloat16)
    key_ref[done : done + slots, :] = rotate(
        total[:, HEADS * HD : (HEADS + 1) * HD], cosine, signed_sine
    ).astype(jnp.bfloat16)
    value_ref[:, done : done + slots] = total[:, (HEADS + 1) * HD :].T.astype(jnp.bfloat16)
    if done + slots < key_ref.shape[0]:
        key_ref[done + slots :, :] = jnp.zeros_like(key_ref[done + slots :, :])
        value_ref[:, done + slots :] = jnp.zeros_like(value_ref[:, done + slots :])


def project(token_pieces, offsets, gain, cosine, signed_sine, weight_pieces, weight_places, done):
    slots = cosine.shape[0]
    width = token_pieces[0].shape[-1]
    blocks = gain.shape[0]
    columns = (HEADS + 2) * HD
    fresh = -(-(done + slots) // KEYS) * KEYS
    whole = pl.BlockSpec(memory_space=pltpu.VMEM)
    remote = pl.BlockSpec(memory_space=pl.ANY)
    scalars = pl.BlockSpec(memory_space=pltpu.SMEM)
    return pl.pallas_call(
        functools.partial(project_kernel, offsets, len(token_pieces), len(weight_pieces), done),
        out_shape=(
            jax.ShapeDtypeStruct((HEADS, slots, HD), jnp.bfloat16),
            jax.ShapeDtypeStruct((fresh, HD), jnp.bfloat16),
            jax.ShapeDtypeStruct((HD, fresh), jnp.bfloat16),
        ),
        in_specs=[scalars, whole, whole, whole]
        + [remote] * (len(token_pieces) + len(weight_pieces)),
        out_specs=(whole, whole, whole),
        scratch_shapes=[
            pltpu.VMEM((blocks, slots, width), jnp.bfloat16),
            pltpu.VMEM((blocks * width, columns), jnp.bfloat16),
            pltpu.VMEM((slots, columns), jnp.float32),
            pltpu.VMEM((slots, HD), jnp.float32),
            pltpu.SemaphoreType.DMA((blocks * len(token_pieces),)),
            pltpu.SemaphoreType.DMA((len(weight_pieces),)),
        ],
        compiler_params=pltpu.CompilerParams(vmem_limit_bytes=48 * 2**20),
        cost_estimate=pl.CostEstimate(
            flops=4 * slots * blocks * width * columns,
            bytes_accessed=2 * blocks * width * (slots + columns),
            transcendentals=0,
        ),
        name="project",
    )(weight_places, gain, cosine, signed_sine, *token_pieces, *weight_pieces)


def attend_slots(
    asked, chosen, stored, slots_seen, keys, values, places, out_ref, peak, denominator, numerator, score_slots
):
    limit = jnp.concatenate([chosen] * HEADS, axis=1)
    peak[...] = jnp.full_like(peak, masked_score)
    denominator[...] = jnp.zeros_like(denominator)
    numerator[...] = jnp.zeros_like(numerator)
    count = stored + (slots_seen + KEYS - 1) // KEYS

    def start_of(block):
        block = jnp.minimum(block, count - 1)
        block = jnp.where(block < stored, block, block - stored + LENGTH // KEYS)
        return pl.multiple_of(block * KEYS, KEYS)

    def score(block, slot):
        score_slots[slot] = lax.dot_general(
            keys[pl.ds(start_of(block), KEYS), :],
            asked,
            (((1,), (1,)), ((), ())),
            preferred_element_type=jnp.float32,
        )

    def gather(block, slot):
        start = start_of(block)
        place = jnp.concatenate([places[pl.ds(start, KEYS), :]] * HEADS, axis=1)
        scores = jnp.where(place <= limit, score_slots[slot], masked_score)
        old_peak = peak[...]
        new_peak = jnp.maximum(old_peak, jnp.max(scores, axis=0, keepdims=True))
        rescale = jnp.exp2((old_peak - new_peak) * exponent_scale)
        exponentials = jnp.exp2((scores - new_peak) * exponent_scale)
        denominator[...] = denominator[...] * rescale + jnp.sum(
            exponentials, axis=0, keepdims=True
        )
        numerator[...] = numerator[...] * rescale + jnp.dot(
            values[:, pl.ds(start, KEYS)],
            exponentials.astype(jnp.bfloat16),
            preferred_element_type=jnp.float32,
        )
        peak[...] = new_peak

    score(0, 0)

    def pair(turn, carry):
        block = 2 * turn
        score(block + 1, 1)
        gather(block, 0)
        score(block + 2, 0)
        gather(block + 1, 1)
        return carry

    lax.fori_loop(0, count // 2, pair, 0)

    @pl.when(count % 2 == 1)
    def _():
        gather(count - 1, 0)

    outcome = jnp.where(limit < LENGTH, numerator[...] / denominator[...], 0.0)
    for head in range(HEADS):
        part = outcome[:, head * SLOTS : (head + 1) * SLOTS]
        out_ref[:, head * HD : (head + 1) * HD] = part.T.astype(jnp.bfloat16)


def attend_kernel(first, blocks_ref, query_ref, chosen_ref, *refs):
    stored_refs, (out_ref, *scratch) = refs[:5], refs[-9:]
    keys, values, places, peak, denominator, numerator, score_slots, sem = scratch
    step = pl.program_id(0)
    fresh = stored_refs[3].shape[0]

    @pl.when(step == 0)
    def _():
        old, new = pl.ds(0, LENGTH), pl.ds(LENGTH, fresh)
        wheres = (keys.at[old, :], values.at[:, old], places, keys.at[new, :], values.at[:, new])
        held_places = stored_refs[2].at[pl.ds(0, LENGTH + fresh), :]
        sources = (*stored_refs[:2], held_places, *stored_refs[3:])
        copies = [
            pltpu.make_async_copy(source, where, sem.at[number])
            for number, (source, where) in enumerate(zip(sources, wheres))
        ]
        for copy in copies:
            copy.start()
        for copy in copies:
            copy.wait()

    attend_slots(
        query_ref[...].reshape(HEADS * SLOTS, HD), chosen_ref[...], blocks_ref[step],
        (first + step + 1) * SLOTS,
        keys, values, places, out_ref, peak, denominator, numerator, score_slots,
    )


def attend(first, key_blocks, queries, chosen, stored, total_slots):
    slots = queries.shape[1]
    rows = HEADS * SLOTS
    length = LENGTH + stored[3].shape[0]
    return pl.pallas_call(
        functools.partial(attend_kernel, first),
        out_shape=jax.ShapeDtypeStruct((total_slots, HEADS * HD), jnp.bfloat16),
        grid_spec=pltpu.PrefetchScalarGridSpec(
            num_scalar_prefetch=1,
            grid=(slots // SLOTS,),
            in_specs=[
                pl.BlockSpec((HEADS, SLOTS, HD), lambda step, counts: (0, step, 0)),
                pl.BlockSpec((1, SLOTS), lambda step, counts: (0, step)),
            ]
            + [pl.BlockSpec(memory_space=pl.ANY)] * 5,
            out_specs=pl.BlockSpec((SLOTS, HEADS * HD), lambda step, counts: (first + step, 0)),
            scratch_shapes=[
                pltpu.VMEM((length, HD), jnp.bfloat16),
                pltpu.VMEM((HD, length), jnp.bfloat16),
                pltpu.VMEM((length, HD), jnp.int32),
                pltpu.VMEM((1, rows), jnp.float32),
                pltpu.VMEM((1, rows), jnp.float32),
                pltpu.VMEM((HD, rows), jnp.float32),
                pltpu.VMEM((2, KEYS, rows), jnp.float32),
                pltpu.SemaphoreType.DMA((5,)),
            ],
        ),
        compiler_params=pltpu.CompilerParams(vmem_limit_bytes=56 * 2**20),
        cost_estimate=pl.CostEstimate(
            flops=slots * HEADS * LENGTH * HD * 2,
            bytes_accessed=12 * 2**20,
            transcendentals=slots * HEADS * LENGTH // 2,
        ),
        name="attend",
    )(key_blocks, queries, chosen, *stored)


def blend_kernel(first, offsets, token_count, weight_count, *refs):
    blocks_ref, weight_place_ref = refs[:2]
    gain_ref, cosine_ref, sine_ref, chosen_ref, old_key_ref, old_value_ref = refs[2:8]
    cache_key_ref, cache_value_ref, cache_place_ref = refs[8:11]
    refs = refs[11:]
    token_refs, refs = refs[:token_count], refs[token_count:]
    weight_refs, refs = refs[:weight_count], refs[weight_count:]
    out_ref, fresh_key_ref, fresh_value_ref, held, weights, total, squares, queries = refs[-18:-10]
    keys, values, places, peak, denominator, numerator, score_slots = refs[-10:-3]
    token_sem, weight_sem, cache_sem = refs[-3:]
    step = pl.program_id(0)
    done = first * SLOTS
    blocks, slots, width = held.shape

    @pl.when(step == 0)
    def _():
        token_copies = []
        for piece, ref in enumerate(token_refs):
            for part in range(ref.shape[0]):
                number = len(token_copies)
                where = held.at[part, pl.ds(offsets[piece], ref.shape[1]), :]
                token_copies.append(pltpu.make_async_copy(ref.at[part], where, token_sem.at[number]))
        weight_copies = []
        for piece, ref in enumerate(weight_refs):
            start = pl.multiple_of(weight_place_ref[piece] * width, width)
            where = weights.at[pl.ds(start, ref.shape[0]), :]
            weight_copies.append(pltpu.make_async_copy(ref, where, weight_sem.at[piece]))
        fresh = fresh_key_ref.shape[0]
        cache_copies = [
            pltpu.make_async_copy(cache_key_ref, keys.at[pl.ds(0, LENGTH), :], cache_sem.at[0]),
            pltpu.make_async_copy(cache_value_ref, values.at[:, pl.ds(0, LENGTH)], cache_sem.at[1]),
            pltpu.make_async_copy(
                cache_place_ref.at[pl.ds(0, LENGTH + fresh), :], places, cache_sem.at[2]
            ),
        ]
        for copy in token_copies:
            copy.start()
        squares[...] = jnp.zeros_like(squares)
        number = 0
        for piece, ref in enumerate(token_refs):
            for block in range(ref.shape[0]):
                if number == len(token_copies) // 4:
                    for copy in weight_copies:
                        copy.start()
                token_copies[number].wait()
                number += 1

                def add_squares(tile, carry, block=block, offset=offsets[piece]):
                    rows = pl.ds(pl.multiple_of(offset + tile * TILE, TILE), TILE)
                    hidden = held[block, rows, :].astype(jnp.float32)
                    hidden = hidden * hidden
                    part = hidden[:, :HD]
                    for start in range(HD, width, HD):
                        part = part + hidden[:, start : start + HD]
                    squares[rows, :] += part
                    return carry

                lax.fori_loop(0, ref.shape[1] // TILE, add_squares, 0)
        mean_square = jnp.sum(squares[...], axis=1, keepdims=True) * (1.0 / (blocks * width))
        squares[...] = jnp.broadcast_to(lax.rsqrt(mean_square + epsilon), squares.shape)
        for copy in weight_copies:
            copy.wait()
        for copy in cache_copies:
            copy.start()
        height = slots // max(1, slots // ROWS)

        def project_rows(tile, carry):
            rows = pl.ds(pl.multiple_of(tile * height, height), height)
            scale = jnp.concatenate([squares[rows, :]] * (width // HD), axis=1)

            def add_blocks(group, carry):
                normed = []
                for part in range(GROUP):
                    block = group * GROUP + part
                    hidden = held[block, rows, :].astype(jnp.float32) * scale
                    normed.append(
                        (hidden * gain_ref[block].astype(jnp.float32)).astype(jnp.bfloat16)
                    )
                depth = GROUP * width
                start = pl.multiple_of(group * depth, depth)
                product = jnp.dot(
                    jnp.concatenate(normed, axis=1),
                    weights[pl.ds(start, depth), :],
                    preferred_element_type=jnp.float32,
                )
                total[rows, :] = jnp.where(group == 0, 0.0, total[rows, :]) + product
                return carry

            return lax.fori_loop(0, blocks // GROUP, add_blocks, carry)

        total[...] = jnp.zeros_like(total)
        lax.fori_loop(0, slots // height, project_rows, 0)
        cosine, signed_sine = cosine_ref[...], sine_ref[...]
        for head in range(HEADS):
            part = total[:, head * HD : (head + 1) * HD]
            queries[head] = rotate(part, cosine, signed_sine).astype(jnp.bfloat16)
        if done:
            fresh_key_ref[:done, :] = old_key_ref[:done, :]
            fresh_value_ref[:, :done] = old_value_ref[:, :done]
        fresh_key_ref[done : done + slots, :] = rotate(
            total[:, HEADS * HD : (HEADS + 1) * HD], cosine, signed_sine
        ).astype(jnp.bfloat16)
        fresh_value_ref[:, done : done + slots] = total[:, (HEADS + 1) * HD :].T.astype(jnp.bfloat16)
        if done + slots < fresh:
            fresh_key_ref[done + slots :, :] = jnp.zeros((fresh - done - slots, HD), jnp.bfloat16)
            fresh_value_ref[:, done + slots :] = jnp.zeros((HD, fresh - done - slots), jnp.bfloat16)
        keys[LENGTH:, :] = fresh_key_ref[...]
        values[:, LENGTH:] = fresh_value_ref[...]
        for copy in cache_copies:
            copy.wait()

    @pl.when(step > 0)
    def _():
        rows = HEADS * SLOTS
        own = pl.ds(pl.multiple_of((step - 1) * SLOTS, SLOTS), SLOTS)
        asked = queries[:, own, :].reshape(rows, HD)
        attend_slots(
            asked, chosen_ref[...], blocks_ref[step - 1], (first + step) * SLOTS,
            keys, values, places, out_ref, peak, denominator, numerator, score_slots,
        )


def blend(
    first, key_blocks, pieces, offsets, weight_pieces, weight_places, gain, cosine,
    signed_sine, chosen, old, keys, values, key_places, total_slots, earlier,
):
    slots = cosine.shape[0]
    width = pieces[0].shape[-1]
    blocks = gain.shape[0]
    columns = (HEADS + 2) * HD
    rows = HEADS * SLOTS
    fresh = -(-(first * SLOTS + slots) // KEYS) * KEYS

    def still(array):
        origin = (0,) * array.ndim
        return pl.BlockSpec(
            array.shape, lambda step, *tables: origin, pipeline_mode=pl.Buffered(1)
        )

    remote = pl.BlockSpec(memory_space=pl.ANY)
    operands = [
        key_blocks, weight_places, gain, cosine, signed_sine, chosen, *old,
        keys, values, key_places, *pieces, *weight_pieces, *earlier,
    ]
    return pl.pallas_call(
        functools.partial(blend_kernel, first, offsets, len(pieces), len(weight_pieces)),
        out_shape=(
            jax.ShapeDtypeStruct((total_slots, HEADS * HD), jnp.bfloat16),
            jax.ShapeDtypeStruct((fresh, HD), jnp.bfloat16),
            jax.ShapeDtypeStruct((HD, fresh), jnp.bfloat16),
        ),
        grid_spec=pltpu.PrefetchScalarGridSpec(
            num_scalar_prefetch=2,
            grid=(1 + slots // SLOTS,),
            in_specs=[
                still(gain),
                still(cosine),
                still(signed_sine),
                pl.BlockSpec((1, SLOTS), lambda step, *tables: (0, jnp.maximum(step - 1, 0))),
                still(old[0]),
                still(old[1]),
            ]
            + [remote] * (3 + len(pieces) + len(weight_pieces) + len(earlier)),
            out_specs=(
                pl.BlockSpec(
                    (SLOTS, HEADS * HD), lambda step, *tables: (first + jnp.maximum(step - 1, 0), 0)
                ),
                pl.BlockSpec((fresh, HD), lambda step, *tables: (0, 0)),
                pl.BlockSpec((HD, fresh), lambda step, *tables: (0, 0)),
            ),
            scratch_shapes=[
                pltpu.VMEM((blocks, slots, width), jnp.bfloat16),
                pltpu.VMEM((blocks * width, columns), jnp.bfloat16),
                pltpu.VMEM((slots, columns), jnp.float32),
                pltpu.VMEM((slots, HD), jnp.float32),
                pltpu.VMEM((HEADS, slots, HD), jnp.bfloat16),
                pltpu.VMEM((LENGTH + fresh, HD), jnp.bfloat16),
                pltpu.VMEM((HD, LENGTH + fresh), jnp.bfloat16),
                pltpu.VMEM((LENGTH + fresh, HD), jnp.int32),
                pltpu.VMEM((1, rows), jnp.float32),
                pltpu.VMEM((1, rows), jnp.float32),
                pltpu.VMEM((HD, rows), jnp.float32),
                pltpu.VMEM((2, KEYS, rows), jnp.float32),
                pltpu.SemaphoreType.DMA((blocks * len(pieces),)),
                pltpu.SemaphoreType.DMA((len(weight_pieces),)),
                pltpu.SemaphoreType.DMA((3,)),
            ],
        ),
        input_output_aliases={len(operands) - 1: 0} if earlier else {},
        compiler_params=pltpu.CompilerParams(vmem_limit_bytes=56 * 2**20),
        cost_estimate=pl.CostEstimate(
            flops=4 * slots * blocks * width * columns + slots * HEADS * LENGTH * HD * 2,
            bytes_accessed=2 * blocks * width * (slots + columns) + 8 * 2**20,
            transcendentals=slots * HEADS * LENGTH // 2,
        ),
        name="blend",
    )(*operands)


def ring(block, axis, shift):
    half = block.shape[-2] // 2
    behind = lax.ppermute(block, axis, shift(1))
    ahead = lax.ppermute(block, axis, shift(-1))
    far_first = lax.ppermute(behind[..., :half, :], axis, shift(1))
    far_second = lax.ppermute(ahead[..., half:, :], axis, shift(-1))
    return [block, behind, ahead, far_first, far_second]


def shards(tokens, norm_gain, w_query, w_keyval, kv_cache, selected, anchor):
    row_index = lax.axis_index("row")
    col_index = lax.axis_index("col")
    own_x, own_core = row_index // 2, row_index % 2
    holds_key = col_index % 2 == 0
    own_cache = kv_cache[0]
    chosen = selected[0]
    slot_count = chosen.shape[0]
    early = EARLY * SLOTS
    middle = NEAR * SPAN
    near_cache = lax.ppermute(own_cache[:middle], "col", flipped(16))
    early_tokens = lax.all_gather(tokens[0, :early], "col", axis=0)
    other_keyval = lax.ppermute(w_keyval, "col", flipped(16))
    late_tokens, other_keyval = lax.optimization_barrier((tokens[0, early:], other_keyval))
    late_tokens = lax.all_gather(late_tokens, "col", axis=0)
    far_cache, early_tokens = lax.optimization_barrier((own_cache[middle:], early_tokens))
    far_cache = lax.ppermute(far_cache, "col", flipped(16))

    weights = jnp.concatenate(
        [
            w_query,
            jnp.where(holds_key, w_keyval, other_keyval),
            jnp.where(holds_key, other_keyval, w_keyval),
        ],
        axis=1,
    )
    mine = ring(weights, "row", row_shift)
    theirs = [lax.ppermute(piece, "row", flipped(8)) for piece in mine]
    steps_x = jnp.array([0, 3, 1, 2, 2], jnp.int32)
    second_half = jnp.array([0, 0, 0, 0, 1], jnp.int32)
    source_x = (own_x + steps_x) % 4
    weight_places = jnp.concatenate(
        [
            (source_x * 2 + own_core) * 2 + second_half,
            (source_x * 2 + 1 - own_core) * 2 + second_half,
        ]
    )

    cosine, signed_sine = angles(chosen.astype(jnp.float32), HD)
    span_starts = jnp.arange(NCHUNK, dtype=jnp.int32) * SPAN - anchor[0]
    span_cosine, span_sine = angles(span_starts.astype(jnp.float32), HD)
    prepared = ()
    for first_span, partner in ((0, near_cache), (NEAR, far_cache)):
        prepared = prepare(
            first_span,
            holds_key.astype(jnp.int32)[None],
            own_cache,
            partner,
            span_cosine[:, None],
            span_sine[:, None],
            prepared,
        )
    keys, values = prepared
    padded = -(-slot_count // KEYS) * KEYS - slot_count
    key_places = mark(jnp.pad(chosen[None], ((0, 0), (0, padded)), constant_values=HIDDEN_POSITION))
    grouped = chosen.reshape(-1, SLOTS)
    farthest = jnp.max(jnp.where(grouped < LENGTH, grouped, -1), axis=1)
    key_blocks = (farthest + KEYS) // KEYS
    gain = norm_gain.reshape(NCHUNK, 1, -1)
    queries, *fresh = project(
        [early_tokens],
        (0,),
        gain,
        cosine[:early],
        signed_sine[:early],
        mine + theirs,
        weight_places,
        0,
    )
    attended = attend(
        0,
        key_blocks[:EARLY],
        queries,
        chosen[None, :early],
        (keys, values, key_places, *fresh),
        slot_count,
    )
    attended, late_tokens = lax.optimization_barrier((attended, late_tokens))
    attended, *_ = blend(
        EARLY,
        key_blocks[EARLY:],
        [late_tokens],
        (0,),
        mine + theirs,
        weight_places,
        gain,
        cosine[early:],
        signed_sine[early:],
        chosen[None, early:],
        fresh,
        keys,
        values,
        key_places,
        slot_count,
        (attended,),
    )
    return attended[None]


def solution(mesh):
    in_specs = (
        P("row", None, "col"),
        P(),
        P("row", "col"),
        P("row", "col"),
        P("row", None, "col"),
        P("row", None),
        P("row", None),
    )
    out_specs = P("row", None, "col")
    return jax.shard_map(shards, mesh=mesh, in_specs=in_specs, out_specs=out_specs, check_vma=False)
```
